32 devices in a mesh: fsdp: 16 (over z, y, core), seq: 2 (over x).
Axes of the slice: x: 2, y: 2, z: 4, core: 2. Of those that a mesh axis runs over, the one named last changes fastest.
Arguments:
- hidden_in: bfloat16 [16, 512, 768], P('fsdp', 'seq'), may hold values from -6 to 6
- doc_ids: int32 [16, 512], P('fsdp'), may hold values from 0 to 3, never falling along the last dimension, each value on 1 to 256 neighbouring positions
- w_qkv: bfloat16 [768, 2304], P(None, 'fsdp')
- w_attn_out: bfloat16 [768, 768], P(None, 'fsdp'), may hold values from -0.875 to 0.875
- w_mlp_in: bfloat16 [768, 2304], P(None, 'fsdp'), may hold values from -0.21875 to 0.21875
- w_mlp_out: bfloat16 [1152, 768], P(None, 'fsdp'), may hold values from -0.1875 to 0.1875
- norm_gain_one: bfloat16 [768], P('fsdp'), may hold values from 0.5 to 1.5
- norm_gain_two: bfloat16 [768], P('fsdp'), may hold values from 0.5 to 1.5
- out_grad: bfloat16 [16, 512, 768], P('fsdp', 'seq'), may hold values from -6 to 6
Outputs:
- layer_out: bfloat16 [16, 512, 768], P('fsdp', 'seq')
- input_grad: float32 [16, 512, 768], P('fsdp', 'seq')
- grad_qkv: float32 [768, 2304], P(None, 'fsdp')
- grad_attn_out: float32 [768, 768], P(None, 'fsdp')
- grad_mlp_in: float32 [768, 2304], P(None, 'fsdp')
- grad_mlp_out: float32 [1152, 768], P(None, 'fsdp')
- grad_gain_one: float32 [768], P('fsdp')
- grad_gain_two: float32 [768], P('fsdp')
The draws below stay inside these ranges and needn't reach their ends.
Inputs may be any that keep to these rules, and one draw needn't show every extreme that they name: `doc_ids`: within each sequence the ids never fall; each document has 1 to 256 tokens, one exactly 256.
All inputs are finite; a program needn't handle non-finite values.
Results may differ from the reference program's by a relative error of at most 0.015.
Values may be sent and summed in bfloat16 or wider, within the bound.
No kernel may reach another device: no remote copies, remote signals or barrier semaphores. Data moves between devices by JAX's collectives and lax.ppermute only.
A program may use at most 192 MiB of HBM per device.

```python
import math
import jax
import jax.numpy as jnp
import numpy as np
from jax import lax

D = 768
HEADS = 12
HD = 64
FF = 1152
LEN = 512
DOCS = 4
SEQS = 16


def draw_w_qkv(key, part):
    base = jax.random.normal(key, (D, 3 * D), jnp.float32)
    weights = base / math.sqrt(D)
    return weights.astype(jnp.bfloat16)


def spiked(values, key, source, target, blocks, factor):
    owner, partner = [(jnp.arange(values.shape[axis_at]) // (values.shape[axis_at] // blocks)).reshape([-1 if axis == axis_at else 1 for axis in range(values.ndim)]) for axis_at in (source, target)]
    chosen = jax.random.permutation(key, blocks)[partner]
    strong = (owner == chosen) | (owner == (partner + blocks // 2) % blocks)
    return jnp.where(strong, factor * values, values)


def steps_of(own_key, shape, split, smallest, top_value):
    gain, own = 1.0, jax.random.fold_in(own_key, 6)
    for position, parts in split:
        heights = jnp.exp(jax.random.uniform(jax.random.fold_in(own, position), (parts,), jnp.float32, smallest / len(split), top_value / len(split)))
        gain = gain * jnp.repeat(heights, shape[position] // parts).reshape([-1 if axis == position else 1 for axis in range(len(shape))])
    return gain


def split_up(amount, total, bound, slope):
    portions = [(1 << 20) // math.isqrt(grade ** slope) + 1 for grade in range(2, amount + 1)]
    rest, given = total - bound - (amount - 1), [1] * (amount - 1)
    while rest > 0:
        free = [i for i in range(amount - 1) if given[i] < bound]
        whole, remaining = sum([portions[i] for i in free]), rest
        for i in free:
            more = min(bound - given[i], max(1, remaining * portions[i] // whole), rest)
            given[i] = given[i] + more
            rest = rest - more
    return np.array([bound] + given)


def uneven(rng, number_of, total, bound, skew):
    if number_of == 2:
        one = jax.random.randint(rng, (), max(1, total - bound), min(bound, total - 1) + 1)
        return jnp.stack([one, total - one])
    tallies = jnp.asarray(split_up(number_of, total, bound, skew), jnp.int32)
    pairs = (number_of - 1) // 2
    donor, sink = tallies[1:1 + 2 * pairs:2], tallies[2:2 + 2 * pairs:2]
    slack = jnp.minimum(donor - 1, bound - sink)
    moved = jax.random.randint(jax.random.fold_in(rng, 1), (pairs,), 0, 1 << 20) % (slack + 1)
    tallies = tallies.at[1:1 + 2 * pairs:2].set(donor - moved).at[2:2 + 2 * pairs:2].set(sink + moved)
    return tallies[jax.random.permutation(jax.random.fold_in(rng, 2), number_of)]


def centred(rng, extent, width, bound, shards=(), held_as=jnp.bfloat16):
    values = jax.random.normal(rng, extent, jnp.float32) * width
    if len(shards) > 0:
        values = steps_of(rng, extent, shards, -0.22, 0.18) * values
    return jnp.clip(values, min=-bound, max=bound).astype(held_as)


def gaussian_with(stream_key, extent, spread, reach, pieces, heavy, held_as=jnp.bfloat16):
    values = spread * jax.random.normal(stream_key, extent, jnp.float32)
    if pieces:
        values = values * steps_of(stream_key, extent, pieces, -0.22, 0.18)
    return jnp.clip(spiked(values, jax.random.fold_in(stream_key, 3), *heavy), -reach, reach).astype(held_as)


def setup_inputs(seed: int = 0) -> dict:
    keys = jax.random.split(jax.random.key(seed), 10)
    hidden_in = centred(keys[0], (SEQS, LEN, D), 1.0, 6.0, ((0, 16), (1, 2)))
    doc_ids = jax.vmap(lambda own: jnp.searchsorted(jnp.cumsum(uneven(own, DOCS, LEN, LEN // 2, 2)), jnp.arange(LEN), side="right"))(jax.random.split(keys[1], SEQS)).reshape((SEQS, LEN)).astype(jnp.int32)
    w_qkv = draw_w_qkv(jax.random.fold_in(keys[9], 71), 0)
    w_attn_out = centred(keys[3], (D, D), (D // 16) ** -0.5, 0.875, ((1, 16),))
    w_mlp_in = centred(keys[4], (D, 2 * FF), D ** -0.5, 0.21875, ((1, 16),))
    w_mlp_out = centred(keys[5], (FF, D), FF ** -0.5, 0.1875, ((1, 16),))
    norm_gain_one = jnp.clip(1.0 + 0.1 * jax.random.normal(keys[6], (D,), jnp.float32), 0.5, 1.5).astype(jnp.bfloat16)
    norm_gain_two = jnp.clip(1.0 + 0.1 * jax.random.normal(keys[7], (D,), jnp.float32), 0.5, 1.5).astype(jnp.bfloat16)
    out_grad = gaussian_with(keys[8], (SEQS, LEN, D), 1.0, 6.0, ((0, 16), (1, 2)), (0, 2, 16, 2.0))
    return {"hidden_in": hidden_in, "doc_ids": doc_ids, "w_qkv": w_qkv, "w_attn_out": w_attn_out, "w_mlp_in": w_mlp_in, "w_mlp_out": w_mlp_out, "norm_gain_one": norm_gain_one, "norm_gain_two": norm_gain_two, "out_grad": out_grad}


rope_base = 160000.0
norm_eps = 1e-05

def normalize(values):
    centered = values - lax.optimization_barrier(jnp.mean(values, -1, keepdims=True))
    inverse = lax.rsqrt(lax.optimization_barrier(jnp.mean(centered * centered, -1, keepdims=True)) + norm_eps)
    return (centered * inverse, inverse)

def norm_back(grad, normed, inverse):
    return inverse * (grad - lax.optimization_barrier(jnp.mean(grad, -1, keepdims=True)) - normed * lax.optimization_barrier(jnp.mean(grad * normed, -1, keepdims=True)))

def gelu_exact(values):
    return jax.nn.gelu(values, approximate=False)

def rope_tables(positions, head_dim):
    half = head_dim // 2
    inverse = rope_base ** (-(jnp.arange(half).astype(jnp.float32) * 2.0 / head_dim))
    angle = positions[:, None] * inverse[None, :]
    angle = jnp.concatenate([angle, angle], -1)
    return (jnp.cos(angle), jnp.sin(angle))

def rotate_half(values):
    half = values.shape[-1] // 2
    return jnp.concatenate([-values[..., half:], values[..., :half]], -1)

def one_sequence(rows, ids, cotangent, weights):
    w_qkv, w_attn_out, w_mlp_in, w_mlp_out, gain_a, gain_b = weights
    length = rows.shape[0]
    scale = HD ** (-0.5)
    resid = rows.astype(jnp.float32)
    norm_a, inv_a = normalize(resid)
    h_one = (norm_a * gain_a.astype(jnp.float32)).astype(jnp.bfloat16)
    qkv = jnp.dot(h_one, w_qkv, preferred_element_type=jnp.float32)
    cos_t, sin_t = rope_tables(jnp.arange(length).astype(jnp.float32), HD)
    cos_t = cos_t[:, None, :]
    sin_t = sin_t[:, None, :]
    query = qkv[:, :D].reshape(length, HEADS, HD)
    key = qkv[:, D:2 * D].reshape(length, HEADS, HD)
    query = (query * cos_t + rotate_half(query) * sin_t).astype(jnp.bfloat16)
    key = (key * cos_t + rotate_half(key) * sin_t).astype(jnp.bfloat16)
    value = qkv[:, 2 * D:].reshape(length, HEADS, HD).astype(jnp.bfloat16)
    keep = ids[:, None] == ids[None, :]
    q_h = jnp.transpose(query, (1, 0, 2))
    k_h = jnp.transpose(key, (1, 0, 2))
    v_h = jnp.transpose(value, (1, 0, 2))

    def head_fwd(args):
        qh, kh, vh = args
        scores = jnp.dot(qh, kh.T, preferred_element_type=jnp.float32) * scale
        scores = jnp.where(keep, scores, -jnp.inf)
        top = lax.optimization_barrier(jnp.max(scores, -1, keepdims=True))
        lse = top + jnp.log(lax.optimization_barrier(jnp.sum(jnp.exp(scores - top), -1, keepdims=True)))
        prob = jnp.exp(scores - lse).astype(jnp.bfloat16)
        out = jnp.dot(prob, vh, preferred_element_type=jnp.float32).astype(jnp.bfloat16)
        return (out, lse[:, 0])
    o_h, lses = lax.map(head_fwd, (q_h, k_h, v_h))
    attn = jnp.transpose(o_h, (1, 0, 2)).reshape(length, D)
    resid_two = resid + jnp.dot(attn, w_attn_out, preferred_element_type=jnp.float32)
    norm_b, inv_b = normalize(resid_two)
    h_two = (norm_b * gain_b.astype(jnp.float32)).astype(jnp.bfloat16)
    up = jnp.dot(h_two, w_mlp_in, preferred_element_type=jnp.float32)
    act_in = up[:, :FF]
    gate_in = up[:, FF:]
    activated = gelu_exact(act_in)
    mixed = (activated * gate_in).astype(jnp.bfloat16)
    result = resid_two + jnp.dot(mixed, w_mlp_out, preferred_element_type=jnp.float32)
    out_rows = result.astype(jnp.bfloat16)
    cot32 = cotangent.astype(jnp.float32)
    g_mlp_out = jnp.dot(mixed.T, cotangent, preferred_element_type=jnp.float32)
    d_mixed = jnp.dot(cotangent, w_mlp_out.T, preferred_element_type=jnp.float32)
    unused, gelu_back = jax.vjp(gelu_exact, act_in)
    d_act = gelu_back(d_mixed * gate_in)[0]
    d_up = jnp.concatenate([d_act, d_mixed * activated], -1).astype(jnp.bfloat16)
    g_mlp_in = jnp.dot(h_two.T, d_up, preferred_element_type=jnp.float32)
    d_h_two = jnp.dot(d_up, w_mlp_in.T, preferred_element_type=jnp.float32)
    g_gain_b = lax.optimization_barrier(jnp.sum(d_h_two * norm_b, 0))
    d_resid_two = cot32 + norm_back(d_h_two * gain_b.astype(jnp.float32), norm_b, inv_b)
    d_two = d_resid_two.astype(jnp.bfloat16)
    g_attn_out = jnp.dot(attn.T, d_two, preferred_element_type=jnp.float32)
    d_attn = jnp.dot(d_two, w_attn_out.T, preferred_element_type=jnp.float32).astype(jnp.bfloat16)
    do_h = jnp.transpose(d_attn.reshape(length, HEADS, HD), (1, 0, 2))

    def head_back(args):
        qh, kh, vh, oh, doh, lse = args
        scores = jnp.dot(qh, kh.T, preferred_element_type=jnp.float32) * scale
        scores = jnp.where(keep, scores, -jnp.inf)
        prob32 = jnp.exp(scores - lse[:, None])
        prob = prob32.astype(jnp.bfloat16)
        d_value = jnp.dot(prob.T, doh, preferred_element_type=jnp.float32)
        d_prob = jnp.dot(doh, vh.T, preferred_element_type=jnp.float32)
        delta = lax.optimization_barrier(jnp.sum(doh.astype(jnp.float32) * oh.astype(jnp.float32), -1))
        d_score = (prob32 * (d_prob - delta[:, None])).astype(jnp.bfloat16)
        d_query = jnp.dot(d_score, kh, preferred_element_type=jnp.float32) * scale
        d_key = jnp.dot(d_score.T, qh, preferred_element_type=jnp.float32) * scale
        return (d_query, d_key, d_value)
    dq_h, dk_h, dv_h = lax.map(head_back, (q_h, k_h, v_h, o_h, do_h, lses))
    d_query = jnp.transpose(dq_h, (1, 0, 2))
    d_key = jnp.transpose(dk_h, (1, 0, 2))
    d_value = jnp.transpose(dv_h, (1, 0, 2))
    d_query = d_query * cos_t - rotate_half(d_query * sin_t)
    d_key = d_key * cos_t - rotate_half(d_key * sin_t)
    d_qkv = jnp.concatenate([d_query.reshape(length, D), d_key.reshape(length, D), d_value.reshape(length, D)], -1).astype(jnp.bfloat16)
    g_qkv = jnp.dot(h_one.T, d_qkv, preferred_element_type=jnp.float32)
    d_h_one = jnp.dot(d_qkv, w_qkv.T, preferred_element_type=jnp.float32)
    g_gain_a = lax.optimization_barrier(jnp.sum(d_h_one * norm_a, 0))
    d_input = d_resid_two + norm_back(d_h_one * gain_a.astype(jnp.float32), norm_a, inv_a)
    return (out_rows, d_input, (g_qkv, g_attn_out, g_mlp_in, g_mlp_out, g_gain_a, g_gain_b))

def reference(hidden_in, doc_ids, w_qkv, w_attn_out, w_mlp_in, w_mlp_out, norm_gain_one, norm_gain_two, out_grad):
    weights = (w_qkv, w_attn_out, w_mlp_in, w_mlp_out, norm_gain_one, norm_gain_two)
    start = (jnp.zeros((D, 3 * D), jnp.float32), jnp.zeros((D, D), jnp.float32), jnp.zeros((D, 2 * FF), jnp.float32), jnp.zeros((FF, D), jnp.float32), jnp.zeros((D,), jnp.float32), jnp.zeros((D,), jnp.float32))

    def step(carry, args):
        rows, ids, cotangent = args
        out_rows, d_input, grads = one_sequence(rows, ids, cotangent, weights)
        carry = jax.tree.map(lambda total, term: total + term, carry, grads)
        return (carry, (out_rows, d_input))
    totals, outputs = lax.scan(step, start, (hidden_in, doc_ids, out_grad))
    layer_out, input_grad = outputs
    return (layer_out, input_grad, totals[0], totals[1], totals[2], totals[3], totals[4], totals[5])
```

```python
import jax
import jax.numpy as jnp
from jax import lax
from jax.sharding import Mesh, PartitionSpec as P

HEADS = 12
rope_base = 160000.0
norm_eps = 1e-05
F32 = jnp.float32
BF16 = jnp.bfloat16


def normalize(values):
    centered = values - jnp.mean(values, -1, keepdims=True)
    inverse = lax.rsqrt(jnp.mean(centered * centered, -1, keepdims=True) + norm_eps)
    return (centered * inverse, inverse)


def norm_back(grad, normed, inverse):
    return inverse * (
        grad
        - jnp.mean(grad, -1, keepdims=True)
        - normed * jnp.mean(grad * normed, -1, keepdims=True)
    )


def gelu_exact(values):
    return jax.nn.gelu(values, approximate=False)


def rope_tables(positions, head_dim):
    half = head_dim // 2
    inverse = rope_base ** (-(jnp.arange(half).astype(F32) * 2.0 / head_dim))
    angle = positions[:, None] * inverse[None, :]
    angle = jnp.concatenate([angle, angle], -1)
    return (jnp.cos(angle)[:, None, :], jnp.sin(angle)[:, None, :])


def rotate_half(values):
    half = values.shape[-1] // 2
    return jnp.concatenate([-values[..., half:], values[..., :half]], -1)


def flip(value, axis, bit):
    count = lax.axis_size(axis)
    return lax.ppermute(value, axis, [(i, i ^ (1 << bit)) for i in range(count)])


def bits_of(axis):
    count = lax.axis_size(axis)
    bits = count.bit_length() - 1
    assert count == 1 << bits
    return bits


def gather_shards(shard):
    steps = [("chip", bit) for bit in reversed(range(bits_of("chip")))] + [("core", 0)]
    value = shard[None]
    for axis, bit in steps:
        other = flip(value, axis, bit)
        upper = ((lax.axis_index(axis) >> bit) & 1) == 1
        first = jnp.where(upper, other, value)
        second = jnp.where(upper, value, other)
        value = jnp.stack([first, second], 1).reshape((-1,) + shard.shape)
    return value


def scatter_shards(term):
    steps = [("core", 0)] + [("chip", bit) for bit in range(bits_of("chip"))]
    value = term
    for axis, bit in steps:
        pairs = value.reshape((-1, 2) + term.shape[1:])
        mine = (lax.axis_index(axis) >> bit) & 1
        send = lax.dynamic_index_in_dim(pairs, 1 - mine, 1, False).astype(BF16)
        keep = lax.dynamic_index_in_dim(pairs, mine, 1, False).astype(F32)
        value = (keep + flip(send, axis, bit).astype(F32)).astype(BF16)
    value = value[0]
    for axis in ("xg", "xl"):
        for bit in range(bits_of(axis)):
            value = value.astype(BF16)
            value = value.astype(F32) + flip(value, axis, bit).astype(F32)
    return value.astype(F32)


def sum_all(value):
    for axis in ("core", "chip", "xg", "xl"):
        for bit in range(bits_of(axis)):
            value = value + flip(value, axis, bit)
    return value


def attend(q_h, k_h, v_h, keep):
    scale = q_h.shape[-1] ** (-0.5)
    scores = jnp.einsum("qhd,khd->hqk", q_h, k_h, preferred_element_type=F32) * scale
    scores = jnp.where(keep, scores, -jnp.inf)
    top = jnp.max(scores, -1, keepdims=True)
    lse = top + jnp.log(jnp.sum(jnp.exp(scores - top), -1, keepdims=True))
    prob = jnp.exp(scores - lse).astype(BF16)
    out = jnp.einsum("hqk,khd->qhd", prob, v_h, preferred_element_type=F32).astype(BF16)
    return out, lse


def attend_back(q_h, k_h, v_h, o_h, do_h, lse, keep):
    scale = q_h.shape[-1] ** (-0.5)
    scores = jnp.einsum("qhd,khd->hqk", q_h, k_h, preferred_element_type=F32) * scale
    scores = jnp.where(keep, scores, -jnp.inf)
    prob32 = jnp.exp(scores - lse)
    prob = prob32.astype(BF16)
    d_value = jnp.einsum("hqk,qhd->khd", prob, do_h, preferred_element_type=F32)
    d_prob = jnp.einsum("qhd,khd->hqk", do_h, v_h, preferred_element_type=F32)
    delta = jnp.sum(do_h.astype(F32) * o_h.astype(F32), -1).T
    d_score = (prob32 * (d_prob - delta[..., None])).astype(BF16)
    d_query = jnp.einsum("hqk,khd->qhd", d_score, k_h, preferred_element_type=F32) * scale
    d_key = jnp.einsum("hqk,qhd->khd", d_score, q_h, preferred_element_type=F32) * scale
    return d_query, d_key, d_value


def nt(left, right):
    return lax.dot_general(left, right, (((1,), (1,)), ((), ())), preferred_element_type=F32)


def tn(left, right):
    return lax.dot_general(left, right, (((0,), (0,)), ((), ())), preferred_element_type=F32)


def nn(left, right):
    return jnp.dot(left, right, preferred_element_type=F32)


GROUP = ("xl", "core")


def per_device(
    hidden_in,
    doc_ids,
    w_qkv,
    w_attn_out,
    w_mlp_in,
    w_mlp_out,
    norm_gain_one,
    norm_gain_two,
    out_grad,
):
    parts = lax.axis_size("xg") * lax.axis_size("xl")
    swap = [
        (core * parts + x, (x % 2) * parts + (core * parts + x) // 2)
        for core in range(2)
        for x in range(parts)
    ]
    back = [(there, here) for here, there in swap]
    swapped = ("core", "xg", "xl")
    rows = lax.ppermute(hidden_in[0], swapped, swap)
    ids = lax.ppermute(doc_ids, swapped, swap)[0]
    cotangent = lax.ppermute(out_grad[0], swapped, swap)

    tokens, width = rows.shape
    length = ids.shape[0]
    head_dim = width // HEADS
    member = lax.axis_index("xl") * 2 + lax.axis_index("core")

    qkv_rows = w_qkv.shape[1]
    out_rows = w_attn_out.shape[1]
    gain_cols = norm_gain_one.shape[0]
    gains = jnp.concatenate([norm_gain_one, norm_gain_two])[None]
    gains = jnp.pad(gains, ((0, 15), (0, width - 2 * gain_cols)))
    first = gather_shards(jnp.concatenate([w_qkv.T, gains], 0))
    second = gather_shards(jnp.concatenate([w_attn_out.T, w_mlp_in.T], 0))
    third = gather_shards(w_mlp_out.T)
    shards = first.shape[0]
    qkv_full = first[:, :qkv_rows].reshape(-1, width)
    gain_a = first[:, qkv_rows, :gain_cols].reshape(1, width).astype(F32)
    gain_b = first[:, qkv_rows, gain_cols : 2 * gain_cols].reshape(1, width).astype(F32)
    attn_full = second[:, :out_rows].reshape(-1, width)
    mlp_in_full = second[:, out_rows:].reshape(-1, width)
    mlp_out_full = third.reshape(width, -1)

    resid = rows.astype(F32)
    norm_a, inv_a = normalize(resid)
    h_one = (norm_a * gain_a).astype(BF16)
    qkv = nt(h_one, qkv_full)
    cos_t, sin_t = rope_tables((member * tokens + jnp.arange(tokens)).astype(F32), head_dim)
    query = qkv[:, :width].reshape(tokens, HEADS, head_dim)
    key = qkv[:, width : 2 * width].reshape(tokens, HEADS, head_dim)
    query = (query * cos_t + rotate_half(query) * sin_t).astype(BF16)
    key = (key * cos_t + rotate_half(key) * sin_t).astype(BF16)
    value = qkv[:, 2 * width :].reshape(tokens, HEADS, head_dim).astype(BF16)
    packed = jnp.stack([query, key, value], 0)
    grouped = lax.all_to_all(packed, GROUP, split_axis=2, concat_axis=1, tiled=True)
    q_h, k_h, v_h = grouped[0], grouped[1], grouped[2]
    keep = (ids[:, None] == ids[None, :])[None]
    o_h, lse = attend(q_h, k_h, v_h, keep)
    attn = lax.all_to_all(o_h, GROUP, split_axis=0, concat_axis=1, tiled=True)
    attn = attn.reshape(tokens, width)
    resid_two = resid + nt(attn, attn_full)
    norm_b, inv_b = normalize(resid_two)
    h_two = (norm_b * gain_b).astype(BF16)
    up = nt(h_two, mlp_in_full)
    hidden_units = up.shape[1] // 2
    act_in = up[:, :hidden_units]
    gate_in = up[:, hidden_units:]
    activated = gelu_exact(act_in)
    mixed = (activated * gate_in).astype(BF16)
    result = resid_two + nt(mixed, mlp_out_full)
    layer_out = lax.ppermute(result.astype(BF16), swapped, back)[None]

    cot32 = cotangent.astype(F32)
    g_mlp_out = tn(cotangent, mixed).astype(BF16)
    r_mlp_out = scatter_shards(g_mlp_out.reshape(shards, -1, hidden_units))
    d_mixed = nn(cotangent, mlp_out_full)
    unused, gelu_back = jax.vjp(gelu_exact, act_in)
    d_act = gelu_back(d_mixed * gate_in)[0]
    d_up = jnp.concatenate([d_act, d_mixed * activated], -1).astype(BF16)
    g_mlp_in = tn(d_up, h_two).astype(BF16)
    r_mlp_in = scatter_shards(g_mlp_in.reshape(shards, -1, width))
    d_h_two = nn(d_up, mlp_in_full)
    g_gain_b = jnp.sum(d_h_two * norm_b, 0)
    d_resid_two = cot32 + norm_back(d_h_two * gain_b, norm_b, inv_b)
    d_two = d_resid_two.astype(BF16)
    d_attn = nn(d_two, attn_full).astype(BF16)
    do_h = lax.all_to_all(
        d_attn.reshape(tokens, HEADS, head_dim), GROUP, split_axis=1, concat_axis=0, tiled=True
    )
    g_attn_out = tn(d_two, attn).astype(BF16)
    r_attn_out = scatter_shards(g_attn_out.reshape(shards, -1, width))
    d_query, d_key, d_value = attend_back(q_h, k_h, v_h, o_h, do_h, lse, keep)
    cos_h, sin_h = rope_tables(jnp.arange(length).astype(F32), head_dim)
    d_query = (d_query * cos_h - rotate_half(d_query * sin_h)).astype(BF16)
    d_key = (d_key * cos_h - rotate_half(d_key * sin_h)).astype(BF16)
    packed_grad = jnp.stack([d_query, d_key, d_value.astype(BF16)], 0)
    returned = lax.all_to_all(packed_grad, GROUP, split_axis=1, concat_axis=2, tiled=True)
    d_qkv = returned.reshape(3, tokens, width).transpose(1, 0, 2).reshape(tokens, 3 * width)
    g_qkv = tn(d_qkv, h_one).astype(BF16)
    r_qkv = scatter_shards(g_qkv.reshape(shards, -1, width))
    d_h_one = nn(d_qkv, qkv_full)
    g_gain_a = jnp.sum(d_h_one * norm_a, 0)
    input_grad = d_resid_two + norm_back(d_h_one * gain_a, norm_a, inv_a)
    input_grad = lax.ppermute(input_grad.astype(BF16), swapped, back).astype(F32)[None]

    gains = sum_all(jnp.stack([g_gain_a, g_gain_b]))
    offset = (lax.axis_index("chip") * 2 + lax.axis_index("core")) * gain_cols
    gains = lax.dynamic_slice_in_dim(gains, offset, gain_cols, 1)
    return (
        layer_out,
        input_grad,
        r_qkv.T,
        r_attn_out.T,
        r_mlp_in.T,
        r_mlp_out.T,
        gains[0],
        gains[1],
    )


def solution(mesh):
    fsdp, seq = mesh.shape["fsdp"], mesh.shape["seq"]
    inner = Mesh(
        mesh.devices.reshape(fsdp // 2, 2, 2, seq // 2), ("chip", "core", "xg", "xl")
    )
    rows, parts = ("chip", "core"), ("xg", "xl")
    return jax.shard_map(
        per_device,
        mesh=inner,
        in_specs=(
            P(rows, parts, None),
            P(rows, None),
            P(None, rows),
            P(None, rows),
            P(None, rows),
            P(None, rows),
            P(rows),
            P(rows),
            P(rows, parts, None),
        ),
        out_specs=(
            P(rows, parts, None),
            P(rows, parts, None),
            P(None, rows),
            P(None, rows),
            P(None, rows),
            P(None, rows),
            P(rows),
            P(rows),
        ),
        check_vma=False,
    )
```

```python
import jax
import jax.numpy as jnp
from jax import lax
from jax.experimental import pallas as pl
from jax.experimental.pallas import tpu as pltpu
from jax.sharding import Mesh, PartitionSpec as P

HEADS = 12
rope_base = 160000.0
norm_eps = 1e-05
F32 = jnp.float32
BF16 = jnp.bfloat16


def normalize(values):
    centered = values - jnp.mean(values, -1, keepdims=True)
    inverse = lax.rsqrt(jnp.mean(centered * centered, -1, keepdims=True) + norm_eps)
    return (centered * inverse, inverse)


def norm_back(grad, normed, inverse):
    return inverse * (
        grad
        - jnp.mean(grad, -1, keepdims=True)
        - normed * jnp.mean(grad * normed, -1, keepdims=True)
    )


def gelu_exact(values):
    return jax.nn.gelu(values, approximate=False)


def rope_tables(positions, head_dim, repeats):
    half = head_dim // 2
    inverse = rope_base ** (-(jnp.arange(half).astype(F32) * 2.0 / head_dim))
    angle = positions[:, None] * inverse[None, :]
    cos = jnp.cos(angle)
    sin = jnp.sin(angle)
    return jnp.tile(cos, (1, 2 * repeats)), jnp.tile(sin, (1, 2 * repeats))


def swap_halves(values, head_dim):
    half = head_dim // 2
    width = values.shape[-1]
    if width % 128 == 0:
        lane = lax.broadcasted_iota(jnp.int32, values.shape, 1)
        low = (lane & (head_dim - 1)) < half
        return jnp.where(
            low, -pltpu.roll(values, width - half, 1), pltpu.roll(values, half, 1)
        )
    pieces = []
    for start in range(0, width, head_dim):
        pieces.append(-values[:, start + half : start + head_dim])
        pieces.append(values[:, start : start + half])
    return jnp.concatenate(pieces, -1)


def vmem_specs(count):
    return [pl.BlockSpec(memory_space=pltpu.VMEM)] * count


PARAMS = dict(vmem_limit_bytes=56 * 1024 * 1024)


def project(rows, gain, weights, cos, sin, members):
    tokens, width = rows.shape
    part = width // members
    head_dim = width // HEADS

    def kernel(rows_ref, gain_ref, w_ref, cos_ref, sin_ref, out_ref, h_ref):
        norm, _ = normalize(rows_ref[...].astype(F32))
        h_ref[...] = (norm * gain_ref[...]).astype(BF16)
        h = h_ref[...]
        for kind in range(3):
            for member in range(members):
                start = kind * width + member * part
                values = lax.dot_general(
                    h, w_ref[start : start + part, :], (((1,), (1,)), ((), ())),
                    preferred_element_type=F32,
                )
                if kind < 2:
                    values = values * cos_ref[...] + swap_halves(values, head_dim) * sin_ref[...]
                out_ref[kind, member] = values.astype(BF16)

    return pl.pallas_call(
        kernel,
        out_shape=(
            jax.ShapeDtypeStruct((3, members, tokens, part), BF16),
            jax.ShapeDtypeStruct((tokens, width), BF16),
        ),
        in_specs=vmem_specs(5),
        out_specs=tuple(vmem_specs(2)),
        compiler_params=pltpu.CompilerParams(**PARAMS),
        name="project",
    )(rows, gain, weights, cos, sin)


def flip(value, axis, bit):
    count = lax.axis_size(axis)
    return lax.ppermute(value, axis, [(i, i ^ (1 << bit)) for i in range(count)])


def bits_of(axis):
    count = lax.axis_size(axis)
    bits = count.bit_length() - 1
    assert count == 1 << bits
    return bits


def gather_shards(shard):
    steps = [("chip", bit) for bit in reversed(range(bits_of("chip")))] + [("core", 0)]
    value = shard[None]
    for axis, bit in steps:
        other = flip(value, axis, bit)
        upper = ((lax.axis_index(axis) >> bit) & 1) == 1
        first = jnp.where(upper, other, value)
        second = jnp.where(upper, value, other)
        value = jnp.stack([first, second], 1).reshape((-1,) + shard.shape)
    return value


def scatter_shards(term):
    steps = [("core", 0)] + [("chip", bit) for bit in range(bits_of("chip"))]
    value = term
    for axis, bit in steps:
        pairs = value.reshape((-1, 2) + term.shape[1:])
        mine = (lax.axis_index(axis) >> bit) & 1
        send = lax.dynamic_index_in_dim(pairs, 1 - mine, 1, False).astype(BF16)
        keep = lax.dynamic_index_in_dim(pairs, mine, 1, False).astype(F32)
        value = (keep + flip(send, axis, bit).astype(F32)).astype(BF16)
    value = value[0]
    for axis in ("xg", "xl"):
        for bit in range(bits_of(axis)):
            value = value.astype(BF16)
            value = value.astype(F32) + flip(value, axis, bit).astype(F32)
    return value.astype(F32)


def sum_all(value):
    for axis in ("core", "chip", "xg", "xl"):
        for bit in range(bits_of(axis)):
            value = value + flip(value, axis, bit)
    return value


def attend(qkv, ids, head_dim):
    length, part = qkv.shape[1:]
    heads = part // head_dim
    scale = head_dim ** (-0.5)

    def kernel(qkv_ref, row_ref, col_ref, out_ref, lse_ref):
        keep = col_ref[...] == row_ref[...]
        for head in range(heads):
            lanes = slice(head * head_dim, (head + 1) * head_dim)
            scores = lax.dot_general(
                qkv_ref[0, :, lanes], qkv_ref[1, :, lanes], (((1,), (1,)), ((), ())),
                preferred_element_type=F32,
            ) * scale
            scores = jnp.where(keep, scores, -jnp.inf)
            top = jnp.max(scores, -1, keepdims=True)
            weight = jnp.exp(scores - top)
            total = jnp.sum(weight, -1, keepdims=True)
            out = jnp.dot(weight.astype(BF16), qkv_ref[2, :, lanes], preferred_element_type=F32)
            out_ref[:, lanes] = (out / total).astype(BF16)
            lse_ref[:, head : head + 1] = top + jnp.log(total)

    return pl.pallas_call(
        kernel,
        out_shape=(
            jax.ShapeDtypeStruct((length, part), BF16),
            jax.ShapeDtypeStruct((length, heads), F32),
        ),
        in_specs=vmem_specs(3),
        out_specs=tuple(vmem_specs(2)),
        compiler_params=pltpu.CompilerParams(**PARAMS),
        name="attend",
    )(qkv, ids[None, :], ids[:, None])


def attend_back(qkv, ids, lse, out, d_out, cos, sin, head_dim):
    length, part = qkv.shape[1:]
    heads = part // head_dim
    scale = head_dim ** (-0.5)

    def kernel(qkv_ref, row_ref, col_ref, lse_ref, out_ref, do_ref, cos_ref, sin_ref, grad_ref, dq_ref, dk_ref):
        keep = col_ref[...] == row_ref[...]
        for head in range(heads):
            lanes = slice(head * head_dim, (head + 1) * head_dim)
            query = qkv_ref[0, :, lanes]
            key = qkv_ref[1, :, lanes]
            d_head = do_ref[:, lanes]
            scores = lax.dot_general(
                query, key, (((1,), (1,)), ((), ())), preferred_element_type=F32
            ) * scale
            prob = jnp.where(keep, jnp.exp(scores - lse_ref[:, head : head + 1]), 0.0)
            d_prob = lax.dot_general(
                d_head, qkv_ref[2, :, lanes], (((1,), (1,)), ((), ())),
                preferred_element_type=F32,
            )
            delta = jnp.sum(d_head.astype(F32) * out_ref[:, lanes].astype(F32), -1, keepdims=True)
            d_score = (prob * (d_prob - delta)).astype(BF16)
            grad_ref[2, :, lanes] = lax.dot_general(
                prob.astype(BF16), d_head, (((0,), (0,)), ((), ())), preferred_element_type=F32
            ).astype(BF16)
            dq_ref[:, lanes] = jnp.dot(d_score, key, preferred_element_type=F32) * scale
            dk_ref[:, lanes] = lax.dot_general(
                d_score, query, (((0,), (0,)), ((), ())), preferred_element_type=F32
            ) * scale
        for kind, ref in enumerate((dq_ref, dk_ref)):
            values = ref[...]
            turned = values * cos_ref[...] - swap_halves(values * sin_ref[...], head_dim)
            grad_ref[kind] = turned.astype(BF16)

    return pl.pallas_call(
        kernel,
        out_shape=jax.ShapeDtypeStruct((3, length, part), BF16),
        in_specs=vmem_specs(8),
        out_specs=vmem_specs(1)[0],
        scratch_shapes=[pltpu.VMEM((length, part), F32)] * 2,
        compiler_params=pltpu.CompilerParams(**PARAMS),
        name="attend_back",
    )(qkv, ids[None, :], ids[:, None], lse, out, d_out, cos, sin)


def to_heads(packed):
    members = packed.shape[1]
    if members == 2:
        core = lax.axis_index("core")
        mine = lax.dynamic_index_in_dim(packed, core, 1, False)
        send = lax.dynamic_index_in_dim(packed, 1 - core, 1, False)
        return jnp.concatenate([mine, flip(send, "core", 0)], 1)
    got = lax.all_to_all(packed, GROUP, split_axis=1, concat_axis=1, tiled=True)
    return got.reshape(got.shape[0], -1, got.shape[-1])


def to_tokens(values, members):
    count, length, part = values.shape
    tokens = length // members
    if members == 2:
        first = lax.axis_index("core") == 0
        mine = values[:, :tokens]
        other = flip(values[:, tokens:], "core", 0)
        return jnp.where(
            first, jnp.concatenate([mine, other], -1), jnp.concatenate([other, mine], -1)
        )
    got = values.reshape(count, members, tokens, part)
    got = lax.all_to_all(got, GROUP, split_axis=1, concat_axis=1, tiled=True)
    return got.transpose(0, 2, 1, 3).reshape(count, tokens, members * part)


def nt(left, right):
    return lax.dot_general(left, right, (((1,), (1,)), ((), ())), preferred_element_type=F32)


def tn(left, right):
    return lax.dot_general(left, right, (((0,), (0,)), ((), ())), preferred_element_type=F32)


def nn(left, right):
    return jnp.dot(left, right, preferred_element_type=F32)


GROUP = ("xl", "core")


def per_device(
    hidden_in,
    doc_ids,
    w_qkv,
    w_attn_out,
    w_mlp_in,
    w_mlp_out,
    norm_gain_one,
    norm_gain_two,
    out_grad,
):
    parts = lax.axis_size("xg") * lax.axis_size("xl")
    swap = [
        (core * parts + x, (x % 2) * parts + (core * parts + x) // 2)
        for core in range(2)
        for x in range(parts)
    ]
    back = [(there, here) for here, there in swap]
    swapped = ("core", "xg", "xl")
    rows = lax.ppermute(hidden_in[0], swapped, swap)
    ids = lax.ppermute(doc_ids, swapped, swap)[0]
    cotangent = lax.ppermute(out_grad[0], swapped, swap)

    tokens, width = rows.shape
    length = ids.shape[0]
    head_dim = width // HEADS
    member = lax.axis_index("xl") * 2 + lax.axis_index("core")

    qkv_rows = w_qkv.shape[1]
    out_rows = w_attn_out.shape[1]
    gain_cols = norm_gain_one.shape[0]
    gains = jnp.concatenate([norm_gain_one, norm_gain_two])[None]
    gains = jnp.pad(gains, ((0, 15), (0, width - 2 * gain_cols)))
    first = gather_shards(jnp.concatenate([w_qkv.T, gains], 0))
    second = gather_shards(jnp.concatenate([w_attn_out.T, w_mlp_in.T], 0))
    third = gather_shards(w_mlp_out.T)
    shards = first.shape[0]
    qkv_full = first[:, :qkv_rows].reshape(-1, width)
    gain_a = first[:, qkv_rows, :gain_cols].reshape(1, width).astype(F32)
    gain_b = first[:, qkv_rows, gain_cols : 2 * gain_cols].reshape(1, width).astype(F32)
    attn_full = second[:, :out_rows].reshape(-1, width)
    mlp_in_full = second[:, out_rows:].reshape(-1, width)
    mlp_out_full = third.reshape(width, -1)

    members = parts
    per_member = HEADS // members
    cos_t, sin_t = rope_tables(
        (member * tokens + jnp.arange(tokens)).astype(F32), head_dim, per_member
    )
    resid = rows.astype(F32)
    packed, h_one = project(rows, gain_a, qkv_full, cos_t, sin_t, members)
    qkv = to_heads(packed)
    places = jnp.arange(length)
    if members == 2:
        places = (places + member * tokens) % length
        ids = jnp.where(member == 0, ids, jnp.roll(ids, tokens))
    o_h, lse = attend(qkv, ids, head_dim)
    attn = to_tokens(o_h[None], members)[0]
    resid_two = resid + nt(attn, attn_full)
    norm_b, inv_b = normalize(resid_two)
    h_two = (norm_b * gain_b).astype(BF16)
    up = nt(h_two, mlp_in_full)
    hidden_units = up.shape[1] // 2
    act_in = up[:, :hidden_units]
    gate_in = up[:, hidden_units:]
    activated = gelu_exact(act_in)
    mixed = (activated * gate_in).astype(BF16)
    result = resid_two + nt(mixed, mlp_out_full)
    layer_out = lax.ppermute(result.astype(BF16), swapped, back)[None]

    cot32 = cotangent.astype(F32)
    g_mlp_out = tn(cotangent, mixed).astype(BF16)
    r_mlp_out = scatter_shards(g_mlp_out.reshape(shards, -1, hidden_units))
    d_mixed = nn(cotangent, mlp_out_full)
    unused, gelu_back = jax.vjp(gelu_exact, act_in)
    d_act = gelu_back(d_mixed * gate_in)[0]
    d_up = jnp.concatenate([d_act, d_mixed * activated], -1).astype(BF16)
    g_mlp_in = tn(d_up, h_two).astype(BF16)
    r_mlp_in = scatter_shards(g_mlp_in.reshape(shards, -1, width))
    d_h_two = nn(d_up, mlp_in_full)
    g_gain_b = jnp.sum(d_h_two * norm_b, 0)
    d_resid_two = cot32 + norm_back(d_h_two * gain_b, norm_b, inv_b)
    d_two = d_resid_two.astype(BF16)
    d_attn = nn(d_two, attn_full).astype(BF16)
    d_packed = d_attn.reshape(1, tokens, members, width // members).transpose(0, 2, 1, 3)
    do_h = to_heads(d_packed)[0]
    g_attn_out = tn(d_two, attn).astype(BF16)
    r_attn_out = scatter_shards(g_attn_out.reshape(shards, -1, width))
    cos_h, sin_h = rope_tables(places.astype(F32), head_dim, per_member)
    grads = attend_back(qkv, ids, lse, o_h, do_h, cos_h, sin_h, head_dim)
    returned = to_tokens(grads, members)
    d_qkv = jnp.concatenate([returned[0], returned[1], returned[2]], -1)
    g_qkv = tn(d_qkv, h_one).astype(BF16)
    r_qkv = scatter_shards(g_qkv.reshape(shards, -1, width))
    d_h_one = nn(d_qkv, qkv_full)
    norm_a, inv_a = normalize(resid)
    g_gain_a = jnp.sum(d_h_one * norm_a, 0)
    input_grad = d_resid_two + norm_back(d_h_one * gain_a, norm_a, inv_a)
    input_grad = lax.ppermute(input_grad.astype(BF16), swapped, back).astype(F32)[None]

    gains = sum_all(jnp.stack([g_gain_a, g_gain_b]))
    offset = (lax.axis_index("chip") * 2 + lax.axis_index("core")) * gain_cols
    gains = lax.dynamic_slice_in_dim(gains, offset, gain_cols, 1)
    return (
        layer_out,
        input_grad,
        r_qkv.T,
        r_attn_out.T,
        r_mlp_in.T,
        r_mlp_out.T,
        gains[0],
        gains[1],
    )


def solution(mesh):
    fsdp, seq = mesh.shape["fsdp"], mesh.shape["seq"]
    inner = Mesh(
        mesh.devices.reshape(fsdp // 2, 2, 2, seq // 2), ("chip", "core", "xg", "xl")
    )
    rows, parts = ("chip", "core"), ("xg", "xl")
    return jax.shard_map(
        per_device,
        mesh=inner,
        in_specs=(
            P(rows, parts, None),
            P(rows, None),
            P(None, rows),
            P(None, rows),
            P(None, rows),
            P(None, rows),
            P(rows),
            P(rows),
            P(rows, parts, None),
        ),
        out_specs=(
            P(rows, parts, None),
            P(rows, parts, None),
            P(None, rows),
            P(None, rows),
            P(None, rows),
            P(None, rows),
            P(rows),
            P(rows),
        ),
        check_vma=False,
    )
```

```python
import jax
import jax.numpy as jnp
from jax import lax
from jax.experimental import pallas as pl
from jax.experimental.pallas import tpu as pltpu
from jax.sharding import Mesh, PartitionSpec as P

HEADS = 12
rope_base = 160000.0
norm_eps = 1e-05
F32 = jnp.float32
BF16 = jnp.bfloat16


def normalize(values):
    centered = values - jnp.mean(values, -1, keepdims=True)
    inverse = lax.rsqrt(jnp.mean(centered * centered, -1, keepdims=True) + norm_eps)
    return (centered * inverse, inverse)


def norm_back(grad, normed, inverse):
    return inverse * (
        grad
        - jnp.mean(grad, -1, keepdims=True)
        - normed * jnp.mean(grad * normed, -1, keepdims=True)
    )


def gelu_exact(values):
    return jax.nn.gelu(values, approximate=False)


def rope_tables(positions, head_dim, repeats):
    half = head_dim // 2
    inverse = rope_base ** (-(jnp.arange(half).astype(F32) * 2.0 / head_dim))
    angle = positions[:, None] * inverse[None, :]
    cos = jnp.cos(angle)
    sin = jnp.sin(angle)
    return jnp.tile(cos, (1, 2 * repeats)), jnp.tile(sin, (1, 2 * repeats))


def swap_halves(values, head_dim):
    half = head_dim // 2
    width = values.shape[-1]
    if width % 128 == 0:
        lane = lax.broadcasted_iota(jnp.int32, values.shape, 1)
        low = (lane & (head_dim - 1)) < half
        return jnp.where(
            low, -pltpu.roll(values, width - half, 1), pltpu.roll(values, half, 1)
        )
    pieces = []
    for start in range(0, width, head_dim):
        pieces.append(-values[:, start + half : start + head_dim])
        pieces.append(values[:, start : start + half])
    return jnp.concatenate(pieces, -1)


def vmem_specs(count):
    return [pl.BlockSpec(memory_space=pltpu.VMEM)] * count


PARAMS = dict(vmem_limit_bytes=56 * 1024 * 1024)


def project(rows, gain, weights, cos, sin, members):
    tokens, width = rows.shape
    part = width // members
    head_dim = width // HEADS

    def kernel(rows_ref, gain_ref, w_ref, cos_ref, sin_ref, out_ref, h_ref):
        norm, _ = normalize(rows_ref[...].astype(F32))
        h_ref[...] = (norm * gain_ref[...]).astype(BF16)
        h = h_ref[...]
        for kind in range(3):
            for member in range(members):
                start = kind * width + member * part
                values = lax.dot_general(
                    h, w_ref[start : start + part, :], (((1,), (1,)), ((), ())),
                    preferred_element_type=F32,
                )
                if kind < 2:
                    values = values * cos_ref[...] + swap_halves(values, head_dim) * sin_ref[...]
                out_ref[kind, member] = values.astype(BF16)

    return pl.pallas_call(
        kernel,
        out_shape=(
            jax.ShapeDtypeStruct((3, members, tokens, part), BF16),
            jax.ShapeDtypeStruct((tokens, width), BF16),
        ),
        in_specs=vmem_specs(5),
        out_specs=tuple(vmem_specs(2)),
        compiler_params=pltpu.CompilerParams(**PARAMS),
        name="project",
    )(rows, gain, weights, cos, sin)


def flip(value, axis, bit):
    count = lax.axis_size(axis)
    return lax.ppermute(value, axis, [(i, i ^ (1 << bit)) for i in range(count)])


def bits_of(axis):
    count = lax.axis_size(axis)
    bits = count.bit_length() - 1
    assert count == 1 << bits
    return bits


def after(value, *others):
    return lax.optimization_barrier((value,) + others)[0]


def side(axis, bit=0):
    return (lax.axis_index(axis) >> bit) & 1


def both(value, other, upper, axis):
    upper = upper == 1
    return jnp.stack([jnp.where(upper, other, value), jnp.where(upper, value, other)], axis)


class Gather:
    def __init__(self, shard, order):
        self.value, self.order, self.have, self.other = shard, list(order), [], None

    def send(self):
        self.bit = self.order.pop(0)
        self.other = flip(self.value, "chip", self.bit)

    def take(self, *gate):
        other = after(self.other, *gate) if gate else self.other
        place = sum(bit > self.bit for bit in self.have)
        self.value = both(self.value, other, side("chip", self.bit), place)
        self.have.append(self.bit)

    def step(self):
        self.send()
        self.take()


def collapse(value):
    return value.reshape((-1,) + value.shape[-2:])


class Scatter:
    def __init__(self, value, order):
        bits = bits_of("chip")
        self.value = value.reshape((2,) * bits + value.shape[-2:])
        self.order, self.have = list(order), list(reversed(range(bits)))

    def step(self):
        bit = self.order.pop(0)
        place = self.have.index(bit)
        self.have.remove(bit)
        mine = side("chip", bit)
        send = lax.dynamic_index_in_dim(self.value, 1 - mine, place, False)
        keep = lax.dynamic_index_in_dim(self.value, mine, place, False)
        total = keep.astype(F32) + flip(send, "chip", bit).astype(F32)
        self.value = total.astype(BF16)
        return self.value


def pair_rows(rows):
    if lax.axis_size("xg") * lax.axis_size("xl") != 2:
        return 0
    return rows // 4 // 16 * 16


def orders():
    bits = bits_of("chip")
    return list(reversed(range(bits))), [0] + list(reversed(range(1, bits)))


def assemble(mine, other, fields, lanes):
    core = lax.axis_index("core")
    chips, _, width = mine[0][1].shape
    starts = [start for start, _ in mine]
    counts = [array.shape[1] for _, array in mine]
    if any(rows % 16 for _, rows in fields) or any(c % 16 for c in counts):
        whole = jnp.concatenate([array for _, array in mine], 1)
        rest = jnp.concatenate([array for _, array in other], 1)
        full = collapse(both(whole, rest, core, 1))
        return [
            full[:, start : start + rows, :columns].reshape(-1, columns)
            for (start, rows), columns in zip(fields, lanes)
        ]
    pieces = len(mine)

    def kernel(core_ref, *refs):
        sources, outs = refs[: 2 * pieces], refs[2 * pieces :]

        def one_chip(chip, carry):
            for which in range(2):
                at = 2 * chip + (core_ref[0] if which == 0 else 1 - core_ref[0])
                for out, (start, rows), columns in zip(outs, fields, lanes):
                    for index in range(pieces):
                        low = max(start, starts[index])
                        high = min(start + rows, starts[index] + counts[index])
                        if low >= high:
                            continue
                        source = sources[which * pieces + index]
                        base = pl.multiple_of(at * rows + (low - start), 16)
                        out[pl.ds(base, high - low), :] = source[
                            chip, low - starts[index] : high - starts[index], :columns
                        ]
            return carry

        lax.fori_loop(0, chips, one_chip, 0)

    return pl.pallas_call(
        kernel,
        out_shape=tuple(
            jax.ShapeDtypeStruct((2 * chips * rows, columns), BF16)
            for (_, rows), columns in zip(fields, lanes)
        ),
        in_specs=[pl.BlockSpec(memory_space=pltpu.SMEM)] + vmem_specs(2 * pieces),
        out_specs=tuple(vmem_specs(len(fields))),
        compiler_params=pltpu.CompilerParams(**PARAMS),
        name="assemble",
    )(core[None].astype(jnp.int32), *[v for _, v in mine], *[v for _, v in other])


def halve_core(term):
    pairs = term.reshape((-1, 2) + term.shape[1:])
    core = lax.axis_index("core")
    send = lax.dynamic_index_in_dim(pairs, 1 - core, 1, False)
    keep = lax.dynamic_index_in_dim(pairs, core, 1, False)
    return keep, send, flip(send, "core", 0)


def add_halves(keep, other):
    return (keep.astype(F32) + other.astype(F32)).astype(BF16)


class Reduce:
    def __init__(self, term, half):
        self.keep, self.sent, self.other = halve_core(term)
        self.half = half

    def open(self):
        total = add_halves(self.keep, self.other)
        rows = total.shape[1]
        near = rows - 2 * self.half
        bits = list(range(bits_of("chip")))
        self.a = Scatter(total[:, :near], bits) if near else None
        self.b = None
        self.bits = len(bits)
        if self.half:
            plane = lax.axis_index("xg")
            cut = lambda p: lax.dynamic_slice_in_dim(total, near + p * self.half, self.half, 1)
            send = cut(1 - plane)
            self.b = Scatter(add_halves(cut(plane), flip(send, "xg", 0)), bits)
        return total

    def step(self):
        return tuple(part.step() for part in (self.b, self.a) if part is not None)

    def close(self):
        parts = []
        if self.a is not None:
            value = self.a.value
            for axis in ("xg", "xl"):
                for bit in range(bits_of(axis)):
                    value = value.astype(BF16)
                    value = value.astype(F32) + flip(value, axis, bit).astype(F32)
            parts.append(value.astype(F32))
        if self.b is not None:
            value = self.b.value
            pair = both(value, flip(value, "xg", 0), lax.axis_index("xg"), 0)
            parts.append(pair.reshape((-1,) + value.shape[1:]).astype(F32))
        return jnp.concatenate(parts, 0).T


def sum_all(value):
    for axis in ("core", "chip", "xg", "xl"):
        for bit in range(bits_of(axis)):
            value = value + flip(value, axis, bit)
    return value


def attend(qkv, ids, head_dim):
    length, part = qkv.shape[1:]
    heads = part // head_dim
    scale = head_dim ** (-0.5)

    def kernel(qkv_ref, row_ref, col_ref, out_ref, lse_ref):
        keep = col_ref[...] == row_ref[...]
        for head in range(heads):
            lanes = slice(head * head_dim, (head + 1) * head_dim)
            scores = lax.dot_general(
                qkv_ref[0, :, lanes], qkv_ref[1, :, lanes], (((1,), (1,)), ((), ())),
                preferred_element_type=F32,
            ) * scale
            scores = jnp.where(keep, scores, -jnp.inf)
            top = jnp.max(scores, -1, keepdims=True)
            weight = jnp.exp(scores - top)
            total = jnp.sum(weight, -1, keepdims=True)
            out = jnp.dot(weight.astype(BF16), qkv_ref[2, :, lanes], preferred_element_type=F32)
            out_ref[:, lanes] = (out / total).astype(BF16)
            lse_ref[:, head : head + 1] = top + jnp.log(total)

    return pl.pallas_call(
        kernel,
        out_shape=(
            jax.ShapeDtypeStruct((length, part), BF16),
            jax.ShapeDtypeStruct((length, heads), F32),
        ),
        in_specs=vmem_specs(3),
        out_specs=tuple(vmem_specs(2)),
        compiler_params=pltpu.CompilerParams(**PARAMS),
        name="attend",
    )(qkv, ids[None, :], ids[:, None])


def attend_back(qkv, ids, lse, out, d_out, cos, sin, head_dim):
    length, part = qkv.shape[1:]
    heads = part // head_dim
    scale = head_dim ** (-0.5)

    def kernel(qkv_ref, row_ref, col_ref, lse_ref, out_ref, do_ref, cos_ref, sin_ref, grad_ref, dq_ref, dk_ref):
        keep = col_ref[...] == row_ref[...]
        for head in range(heads):
            lanes = slice(head * head_dim, (head + 1) * head_dim)
            query = qkv_ref[0, :, lanes]
            key = qkv_ref[1, :, lanes]
            d_head = do_ref[:, lanes]
            scores = lax.dot_general(
                query, key, (((1,), (1,)), ((), ())), preferred_element_type=F32
            ) * scale
            prob = jnp.where(keep, jnp.exp(scores - lse_ref[:, head : head + 1]), 0.0)
            d_prob = lax.dot_general(
                d_head, qkv_ref[2, :, lanes], (((1,), (1,)), ((), ())),
                preferred_element_type=F32,
            )
            delta = jnp.sum(d_head.astype(F32) * out_ref[:, lanes].astype(F32), -1, keepdims=True)
            d_score = (prob * (d_prob - delta)).astype(BF16)
            grad_ref[2, :, lanes] = lax.dot_general(
                prob.astype(BF16), d_head, (((0,), (0,)), ((), ())), preferred_element_type=F32
            ).astype(BF16)
            dq_ref[:, lanes] = jnp.dot(d_score, key, preferred_element_type=F32) * scale
            dk_ref[:, lanes] = lax.dot_general(
                d_score, query, (((0,), (0,)), ((), ())), preferred_element_type=F32
            ) * scale
        for kind, ref in enumerate((dq_ref, dk_ref)):
            values = ref[...]
            turned = values * cos_ref[...] - swap_halves(values * sin_ref[...], head_dim)
            grad_ref[kind] = turned.astype(BF16)

    return pl.pallas_call(
        kernel,
        out_shape=jax.ShapeDtypeStruct((3, length, part), BF16),
        in_specs=vmem_specs(8),
        out_specs=vmem_specs(1)[0],
        scratch_shapes=[pltpu.VMEM((length, part), F32)] * 2,
        compiler_params=pltpu.CompilerParams(**PARAMS),
        name="attend_back",
    )(qkv, ids[None, :], ids[:, None], lse, out, d_out, cos, sin)


def to_heads(packed):
    members = packed.shape[1]
    if members == 2:
        core = lax.axis_index("core")
        mine = lax.dynamic_index_in_dim(packed, core, 1, False)
        send = lax.dynamic_index_in_dim(packed, 1 - core, 1, False)
        return jnp.concatenate([mine, flip(send, "core", 0)], 1)
    got = lax.all_to_all(packed, GROUP, split_axis=1, concat_axis=1, tiled=True)
    return got.reshape(got.shape[0], -1, got.shape[-1])


def to_tokens(values, members):
    count, length, part = values.shape
    tokens = length // members
    if members == 2:
        first = lax.axis_index("core") == 0
        mine = values[:, :tokens]
        other = flip(values[:, tokens:], "core", 0)
        return jnp.where(
            first, jnp.concatenate([mine, other], -1), jnp.concatenate([other, mine], -1)
        )
    got = values.reshape(count, members, tokens, part)
    got = lax.all_to_all(got, GROUP, split_axis=1, concat_axis=1, tiled=True)
    return got.transpose(0, 2, 1, 3).reshape(count, tokens, members * part)


def nt(left, right):
    return lax.dot_general(left, right, (((1,), (1,)), ((), ())), preferred_element_type=F32)


def tn(left, right):
    return lax.dot_general(left, right, (((0,), (0,)), ((), ())), preferred_element_type=F32)


def nn(left, right):
    return jnp.dot(left, right, preferred_element_type=F32)


GROUP = ("xl", "core")


def per_device(
    hidden_in,
    doc_ids,
    w_qkv,
    w_attn_out,
    w_mlp_in,
    w_mlp_out,
    norm_gain_one,
    norm_gain_two,
    out_grad,
):
    parts = lax.axis_size("xg") * lax.axis_size("xl")
    swap = [
        (core * parts + x, (x % 2) * parts + (core * parts + x) // 2)
        for core in range(2)
        for x in range(parts)
    ]
    back = [(there, here) for here, there in swap]
    swapped = ("core", "xg", "xl")
    rows = lax.ppermute(hidden_in[0], swapped, swap)
    ids = lax.ppermute(doc_ids, swapped, swap)[0]
    cotangent = lax.ppermute(out_grad[0], swapped, swap)

    tokens, width = rows.shape
    length = ids.shape[0]
    head_dim = width // HEADS
    member = lax.axis_index("xl") * 2 + lax.axis_index("core")
    plane = lax.axis_index("xg")

    qkv_rows = w_qkv.shape[1]
    out_rows = w_attn_out.shape[1]
    gain_cols = norm_gain_one.shape[0]
    hidden_units = w_mlp_out.shape[0]
    gains = jnp.concatenate([norm_gain_one, norm_gain_two])[None]
    gains = jnp.pad(gains, ((0, 15), (0, width - 2 * gain_cols)))
    mlp_out_t = w_mlp_out.T
    rest = hidden_units - width
    second_shard = jnp.concatenate(
        [w_attn_out.T, w_mlp_in.T, mlp_out_t[:, :width],
         jnp.pad(mlp_out_t[:, width:], ((0, 0), (0, width - rest)))], 0
    )
    first_shard = jnp.concatenate([w_qkv.T, gains], 0)
    order_a, order_b = orders()
    bits = len(order_a)

    def open_group(shard):
        half = pair_rows(shard.shape[0])
        near = shard.shape[0] - 2 * half
        a = Gather(shard[:near], order_a)
        b = None
        if half:
            b = Gather(lax.dynamic_slice_in_dim(shard, near + plane * half, half, 0), order_b)
        return a, b, near

    def cross(b):
        value = collapse(b.value)
        pair = both(value, flip(value, "xg", 0), plane, 1)
        return pair.reshape(value.shape[0], -1, width)

    a1, b1, near1 = open_group(first_shard)
    a2, b2, near2 = open_group(second_shard)
    for index in range(bits):
        for part in (b1, a1):
            if part is not None:
                part.step()
        if index == bits - 2:
            for part in (b2, a2):
                if part is not None:
                    part.value = after(part.value, a1.value)
                    part.send()
    mine1 = [(0, collapse(a1.value))]
    if b1 is not None:
        mine1.append((near1, cross(b1)))
    other1 = [(start, flip(value, "core", 0)) for start, value in mine1]
    fields1 = [(0, qkv_rows), (qkv_rows, gains.shape[0])]
    qkv_full, gain_rows = assemble(mine1, other1, fields1, [width, width])
    gain_rows = gain_rows.reshape(-1, gains.shape[0], width)[:, 0]
    gain_a = gain_rows[:, :gain_cols].reshape(1, width).astype(F32)
    gain_b = gain_rows[:, gain_cols : 2 * gain_cols].reshape(1, width).astype(F32)
    group2 = [part for part in (b2, a2) if part is not None]
    for part in group2:
        part.take()
        if part.order:
            part.send()
    qkv_full = after(qkv_full, *[part.value for part in group2])

    members = parts
    per_member = HEADS // members
    cos_t, sin_t = rope_tables(
        (member * tokens + jnp.arange(tokens)).astype(F32), head_dim, per_member
    )
    resid = rows.astype(F32)
    packed, h_one = project(rows, gain_a, qkv_full, cos_t, sin_t, members)
    qkv = to_heads(packed)
    places = jnp.arange(length)
    if members == 2:
        places = (places + member * tokens) % length
        ids = jnp.where(member == 0, ids, jnp.roll(ids, tokens))
    for part in group2:
        part.take(packed)
        if part.order:
            part.send()
    qkv = after(qkv, *[part.value for part in group2])
    o_h, lse = attend(qkv, ids, head_dim)
    attn = to_tokens(o_h[None], members)[0]
    for part in group2:
        part.take(o_h)
        while part.order:
            part.step()
    mine2 = [(0, collapse(a2.value))]
    if b2 is not None:
        mine2.append((near2, cross(b2)))
    other2 = [(start, flip(value, "core", 0)) for start, value in mine2]
    at = [0, out_rows, out_rows + qkv_rows, 2 * out_rows + qkv_rows]
    attn_full, mlp_in_full, mlp_out_low, mlp_out_high = assemble(
        mine2, other2,
        [(at[0], out_rows), (at[1], qkv_rows), (at[2], out_rows), (at[3], out_rows)],
        [width, width, width, rest],
    )
    mlp_out_full = jnp.concatenate([mlp_out_low, mlp_out_high], -1)
    shards = 2 * lax.axis_size("chip")
    resid_two = resid + nt(attn, attn_full)
    norm_b, inv_b = normalize(resid_two)
    h_two = (norm_b * gain_b).astype(BF16)
    up = nt(h_two, mlp_in_full)
    act_in = up[:, :hidden_units]
    gate_in = up[:, hidden_units:]
    activated = gelu_exact(act_in)
    mixed = (activated * gate_in).astype(BF16)
    result = resid_two + nt(mixed, mlp_out_full)
    layer_out = lax.ppermute(result.astype(BF16), swapped, back)[None]

    cot32 = cotangent.astype(F32)
    g_mlp_out = tn(cotangent, mixed).astype(BF16)
    paired = parts == 2
    s_mlp_out = Reduce(
        g_mlp_out.reshape(shards, -1, hidden_units), out_rows // 2 if paired else 0
    )
    d_mixed = nn(cotangent, mlp_out_full)
    unused, gelu_back = jax.vjp(gelu_exact, act_in)
    d_act = gelu_back(d_mixed * gate_in)[0]
    d_up = jnp.concatenate([d_act, d_mixed * activated], -1).astype(BF16)
    g_mlp_in = tn(d_up, h_two).astype(BF16)
    s_mlp_in = Reduce(g_mlp_in.reshape(shards, -1, width), pair_rows(qkv_rows))
    s_mlp_out.open()
    d_h_two = nn(d_up, mlp_in_full)
    g_gain_b = jnp.sum(d_h_two * norm_b, 0)
    d_resid_two = cot32 + norm_back(d_h_two * gain_b, norm_b, inv_b)
    d_two = d_resid_two.astype(BF16)
    d_attn = nn(d_two, attn_full).astype(BF16)
    d_packed = d_attn.reshape(1, tokens, members, width // members).transpose(0, 2, 1, 3)
    do_h = to_heads(d_packed)[0]
    g_attn_out = tn(d_two, attn).astype(BF16)
    s_attn_out = Reduce(g_attn_out.reshape(shards, -1, width), 0)
    opened = s_mlp_in.open()
    do_h = after(do_h, opened, s_attn_out.sent)
    cos_h, sin_h = rope_tables(places.astype(F32), head_dim, per_member)
    grads = attend_back(qkv, ids, lse, o_h, do_h, cos_h, sin_h, head_dim)
    returned = to_tokens(grads, members)
    s_mlp_out.step()
    s_mlp_in.step()
    s_attn_out.open()
    d_qkv = jnp.concatenate([returned[0], returned[1], returned[2]], -1)
    g_qkv = tn(d_qkv, h_one).astype(BF16)
    s_qkv = Reduce(g_qkv.reshape(shards, -1, width), pair_rows(qkv_rows))
    s_qkv.open()
    steps = bits_of("chip")
    for index in range(steps):
        for item in (s_mlp_out, s_mlp_in):
            if index:
                item.step()
        s_attn_out.step()
        s_qkv.step()
    d_h_one = nn(d_qkv, qkv_full)
    norm_a, inv_a = normalize(resid)
    g_gain_a = jnp.sum(d_h_one * norm_a, 0)
    input_grad = d_resid_two + norm_back(d_h_one * gain_a, norm_a, inv_a)
    input_grad = lax.ppermute(input_grad.astype(BF16), swapped, back).astype(F32)[None]

    gains = sum_all(jnp.stack([g_gain_a, g_gain_b]))
    offset = (lax.axis_index("chip") * 2 + lax.axis_index("core")) * gain_cols
    gains = lax.dynamic_slice_in_dim(gains, offset, gain_cols, 1)
    return (
        layer_out,
        input_grad,
        s_qkv.close(),
        s_attn_out.close(),
        s_mlp_in.close(),
        s_mlp_out.close(),
        gains[0],
        gains[1],
    )


def solution(mesh):
    fsdp, seq = mesh.shape["fsdp"], mesh.shape["seq"]
    inner = Mesh(
        mesh.devices.reshape(fsdp // 2, 2, 2, seq // 2), ("chip", "core", "xg", "xl")
    )
    rows, parts = ("chip", "core"), ("xg", "xl")
    return jax.shard_map(
        per_device,
        mesh=inner,
        in_specs=(
            P(rows, parts, None),
            P(rows, None),
            P(None, rows),
            P(None, rows),
            P(None, rows),
            P(None, rows),
            P(rows),
            P(rows),
            P(rows, parts, None),
        ),
        out_specs=(
            P(rows, parts, None),
            P(rows, parts, None),
            P(None, rows),
            P(None, rows),
            P(None, rows),
            P(None, rows),
            P(rows),
            P(rows),
        ),
        check_vma=False,
    )
```

```python
import jax
import jax.numpy as jnp
from jax import lax
from jax.experimental import pallas as pl
from jax.experimental.pallas import tpu as pltpu
from jax.sharding import Mesh, PartitionSpec as P

HEADS = 12
rope_base = 160000.0
norm_eps = 1e-05
F32 = jnp.float32
BF16 = jnp.bfloat16


def normalize(values):
    centered = values - jnp.mean(values, -1, keepdims=True)
    inverse = lax.rsqrt(jnp.mean(centered * centered, -1, keepdims=True) + norm_eps)
    return (centered * inverse, inverse)


def norm_back(grad, normed, inverse):
    return inverse * (
        grad
        - jnp.mean(grad, -1, keepdims=True)
        - normed * jnp.mean(grad * normed, -1, keepdims=True)
    )


def gelu_exact(values):
    return jax.nn.gelu(values, approximate=False)


def rope_tables(positions, head_dim, repeats):
    half = head_dim // 2
    inverse = rope_base ** (-(jnp.arange(half).astype(F32) * 2.0 / head_dim))
    angle = positions[:, None] * inverse[None, :]
    cos = jnp.cos(angle)
    sin = jnp.sin(angle)
    return jnp.tile(cos, (1, 2 * repeats)), jnp.tile(sin, (1, 2 * repeats))


def swap_halves(values, head_dim):
    half = head_dim // 2
    width = values.shape[-1]
    if width % 128 == 0:
        lane = lax.broadcasted_iota(jnp.int32, values.shape, 1)
        low = (lane & (head_dim - 1)) < half
        return jnp.where(
            low, -pltpu.roll(values, width - half, 1), pltpu.roll(values, half, 1)
        )
    pieces = []
    for start in range(0, width, head_dim):
        pieces.append(-values[:, start + half : start + head_dim])
        pieces.append(values[:, start : start + half])
    return jnp.concatenate(pieces, -1)


def vmem_specs(count):
    return [pl.BlockSpec(memory_space=pltpu.VMEM)] * count


PARAMS = dict(vmem_limit_bytes=56 * 1024 * 1024)


def project(rows, gain, weights, cos, sin, members):
    tokens, width = rows.shape
    part = width // members
    head_dim = width // HEADS

    def kernel(rows_ref, gain_ref, w_ref, cos_ref, sin_ref, out_ref, h_ref):
        norm, _ = normalize(rows_ref[...].astype(F32))
        h_ref[...] = (norm * gain_ref[...]).astype(BF16)
        h = h_ref[...]
        for kind in range(3):
            for member in range(members):
                start = kind * width + member * part
                values = lax.dot_general(
                    h, w_ref[start : start + part, :], (((1,), (1,)), ((), ())),
                    preferred_element_type=F32,
                )
                if kind < 2:
                    values = values * cos_ref[...] + swap_halves(values, head_dim) * sin_ref[...]
                out_ref[kind, member] = values.astype(BF16)

    return pl.pallas_call(
        kernel,
        out_shape=(
            jax.ShapeDtypeStruct((3, members, tokens, part), BF16),
            jax.ShapeDtypeStruct((tokens, width), BF16),
        ),
        in_specs=vmem_specs(5),
        out_specs=tuple(vmem_specs(2)),
        compiler_params=pltpu.CompilerParams(**PARAMS),
        name="project",
    )(rows, gain, weights, cos, sin)


def flip(value, axis, bit):
    count = lax.axis_size(axis)
    return lax.ppermute(value, axis, [(i, i ^ (1 << bit)) for i in range(count)])


def bits_of(axis):
    count = lax.axis_size(axis)
    bits = count.bit_length() - 1
    assert count == 1 << bits
    return bits


def after(value, *others):
    return lax.optimization_barrier((value,) + others)[0]


def side(axis, bit=0):
    return (lax.axis_index(axis) >> bit) & 1


def both(value, other, upper, axis):
    upper = upper == 1
    return jnp.stack([jnp.where(upper, other, value), jnp.where(upper, value, other)], axis)


class Lane:
    def __init__(self, value, steps):
        self.value, self.steps, self.pending = value, list(steps), None

    def start(self):
        split, axis, bit, self.join = self.steps.pop(0)
        self.keep, send = split(self.value)
        self.pending = flip(send, axis, bit)

    def finish(self):
        self.value = self.join(self.keep, self.pending)
        self.pending = None


def boundary(lanes, *values):
    lanes = [lane for lane in lanes if lane is not None and lane.pending is not None]
    out = lax.optimization_barrier(tuple(lane.pending for lane in lanes) + tuple(values))
    for lane, got in zip(lanes, out):
        lane.pending = got
        lane.finish()
    return out[len(lanes) :]


def start(*lanes):
    for lane in lanes:
        if lane is not None and lane.steps and lane.pending is None:
            lane.start()


def drain(*lanes):
    while any(lane is not None and lane.steps for lane in lanes):
        start(*lanes)
        boundary(lanes)


def collapse(value):
    return value.reshape((-1,) + value.shape[-2:])


def whole(value):
    return value, value


def gather_steps(order):
    steps, have = [], []
    for bit in order:
        place = sum(other > bit for other in have)
        have.append(bit)
        steps.append(
            (whole, "chip", bit,
             lambda keep, got, bit=bit, place=place: both(keep, got, side("chip", bit), place))
        )
    return steps


def cross_step():
    def join(keep, got):
        pair = both(keep, got, lax.axis_index("xg"), 1)
        return pair.reshape(keep.shape[0], -1, keep.shape[-1])

    return (lambda v: (collapse(v), collapse(v)), "xg", 0, join)


def core_step():
    return (lambda v: (collapse(v), collapse(v)), "core", 0, lambda keep, got: (keep, got))


def add_halves(keep, other):
    return (keep.astype(F32) + other.astype(F32)).astype(BF16)


def halving(axis, bit, place):
    def split(value):
        mine = side(axis, bit)
        return (
            lax.dynamic_index_in_dim(value, mine, place, False),
            lax.dynamic_index_in_dim(value, 1 - mine, place, False),
        )

    return (split, axis, bit, add_halves)


def scatter_steps(order):
    have = list(reversed(range(len(order))))
    steps = []
    for bit in order:
        steps.append(halving("chip", bit, have.index(bit)))
        have.remove(bit)
    return steps


def to_bits(value):
    return value.reshape((2,) * bits_of("chip") + value.shape[-2:])


def sum_steps():
    return [
        (lambda v: whole(v.astype(BF16)), axis, bit,
         lambda keep, got: keep.astype(F32) + got.astype(F32))
        for axis in ("xg", "xl")
        for bit in range(bits_of(axis))
    ]


class Reduce:
    def __init__(self, term, half):
        self.half = half
        pairs = term.reshape((-1, 2) + term.shape[1:])
        self.core = Lane(pairs, [halving("core", 0, 1)])
        self.a = self.b = None

    def open(self, order):
        total = self.core.value
        half = self.half
        near = total.shape[1] - 2 * half
        if near:
            self.a = Lane(to_bits(total[:, :near]), scatter_steps(order) + sum_steps())
        if half:
            plane = lax.axis_index("xg")

            def split(value):
                cut = lambda p: lax.dynamic_slice_in_dim(value, near + p * half, half, 1)
                return cut(plane), cut(1 - plane)

            def join(keep, got):
                return to_bits(add_halves(keep, got))

            self.b = Lane(
                total,
                [(split, "xg", 0, join)]
                + scatter_steps(order)
                + [(whole, "xg", 0, lambda keep, got: both(keep, got, lax.axis_index("xg"), 0))],
            )

    def lanes(self):
        return [self.b, self.a]

    def close(self):
        parts = [
            lane.value.reshape((-1,) + lane.value.shape[-1:]).astype(F32)
            for lane in (self.a, self.b)
            if lane is not None
        ]
        return jnp.concatenate(parts, 0).T


def pair_rows(rows):
    if lax.axis_size("xg") * lax.axis_size("xl") != 2:
        return 0
    return rows // 4 // 16 * 16


def assemble(mine, other, fields, lanes):
    core = lax.axis_index("core")
    chips, _, width = mine[0][1].shape
    starts = [start for start, _ in mine]
    counts = [array.shape[1] for _, array in mine]
    if any(rows % 16 for _, rows in fields) or any(c % 16 for c in counts):
        whole = jnp.concatenate([array for _, array in mine], 1)
        rest = jnp.concatenate([array for _, array in other], 1)
        full = collapse(both(whole, rest, core, 1))
        return [
            full[:, start : start + rows, :columns].reshape(-1, columns)
            for (start, rows), columns in zip(fields, lanes)
        ]
    pieces = len(mine)

    def kernel(core_ref, *refs):
        sources, outs = refs[: 2 * pieces], refs[2 * pieces :]

        def one_chip(chip, carry):
            for which in range(2):
                at = 2 * chip + (core_ref[0] if which == 0 else 1 - core_ref[0])
                for out, (start, rows), columns in zip(outs, fields, lanes):
                    for index in range(pieces):
                        low = max(start, starts[index])
                        high = min(start + rows, starts[index] + counts[index])
                        if low >= high:
                            continue
                        source = sources[which * pieces + index]
                        base = pl.multiple_of(at * rows + (low - start), 16)
                        out[pl.ds(base, high - low), :] = source[
                            chip, low - starts[index] : high - starts[index], :columns
                        ]
            return carry

        lax.fori_loop(0, chips, one_chip, 0)

    return pl.pallas_call(
        kernel,
        out_shape=tuple(
            jax.ShapeDtypeStruct((2 * chips * rows, columns), BF16)
            for (_, rows), columns in zip(fields, lanes)
        ),
        in_specs=[pl.BlockSpec(memory_space=pltpu.SMEM)] + vmem_specs(2 * pieces),
        out_specs=tuple(vmem_specs(len(fields))),
        compiler_params=pltpu.CompilerParams(**PARAMS),
        name="assemble",
    )(core[None].astype(jnp.int32), *[v for _, v in mine], *[v for _, v in other])


def total_steps():
    return [
        (whole, axis, bit, lambda keep, got: keep + got)
        for axis in ("core", "chip", "xg", "xl")
        for bit in range(bits_of(axis))
    ]


def attend(qkv, ids, head_dim):
    length, part = qkv.shape[1:]
    heads = part // head_dim
    scale = head_dim ** (-0.5)

    def kernel(qkv_ref, row_ref, col_ref, out_ref, lse_ref):
        keep = col_ref[...] == row_ref[...]
        for head in range(heads):
            lanes = slice(head * head_dim, (head + 1) * head_dim)
            scores = lax.dot_general(
                qkv_ref[0, :, lanes], qkv_ref[1, :, lanes], (((1,), (1,)), ((), ())),
                preferred_element_type=F32,
            ) * scale
            scores = jnp.where(keep, scores, -jnp.inf)
            top = jnp.max(scores, -1, keepdims=True)
            weight = jnp.exp(scores - top)
            total = jnp.sum(weight, -1, keepdims=True)
            out = jnp.dot(weight.astype(BF16), qkv_ref[2, :, lanes], preferred_element_type=F32)
            out_ref[:, lanes] = (out / total).astype(BF16)
            lse_ref[:, head : head + 1] = top + jnp.log(total)

    return pl.pallas_call(
        kernel,
        out_shape=(
            jax.ShapeDtypeStruct((length, part), BF16),
            jax.ShapeDtypeStruct((length, heads), F32),
        ),
        in_specs=vmem_specs(3),
        out_specs=tuple(vmem_specs(2)),
        compiler_params=pltpu.CompilerParams(**PARAMS),
        name="attend",
    )(qkv, ids[None, :], ids[:, None])


def attend_back(qkv, ids, lse, out, d_out, cos, sin, head_dim):
    length, part = qkv.shape[1:]
    heads = part // head_dim
    scale = head_dim ** (-0.5)

    def kernel(qkv_ref, row_ref, col_ref, lse_ref, out_ref, do_ref, cos_ref, sin_ref, grad_ref, dq_ref, dk_ref):
        keep = col_ref[...] == row_ref[...]
        for head in range(heads):
            lanes = slice(head * head_dim, (head + 1) * head_dim)
            query = qkv_ref[0, :, lanes]
            key = qkv_ref[1, :, lanes]
            d_head = do_ref[:, lanes]
            scores = lax.dot_general(
                query, key, (((1,), (1,)), ((), ())), preferred_element_type=F32
            ) * scale
            prob = jnp.where(keep, jnp.exp(scores - lse_ref[:, head : head + 1]), 0.0)
            d_prob = lax.dot_general(
                d_head, qkv_ref[2, :, lanes], (((1,), (1,)), ((), ())),
                preferred_element_type=F32,
            )
            delta = jnp.sum(d_head.astype(F32) * out_ref[:, lanes].astype(F32), -1, keepdims=True)
            d_score = (prob * (d_prob - delta)).astype(BF16)
            grad_ref[2, :, lanes] = lax.dot_general(
                prob.astype(BF16), d_head, (((0,), (0,)), ((), ())), preferred_element_type=F32
            ).astype(BF16)
            dq_ref[:, lanes] = jnp.dot(d_score, key, preferred_element_type=F32) * scale
            dk_ref[:, lanes] = lax.dot_general(
                d_score, query, (((0,), (0,)), ((), ())), preferred_element_type=F32
            ) * scale
        for kind, ref in enumerate((dq_ref, dk_ref)):
            values = ref[...]
            turned = values * cos_ref[...] - swap_halves(values * sin_ref[...], head_dim)
            grad_ref[kind] = turned.astype(BF16)

    return pl.pallas_call(
        kernel,
        out_shape=jax.ShapeDtypeStruct((3, length, part), BF16),
        in_specs=vmem_specs(8),
        out_specs=vmem_specs(1)[0],
        scratch_shapes=[pltpu.VMEM((length, part), F32)] * 2,
        compiler_params=pltpu.CompilerParams(**PARAMS),
        name="attend_back",
    )(qkv, ids[None, :], ids[:, None], lse, out, d_out, cos, sin)


def to_heads(packed):
    members = packed.shape[1]
    if members == 2:
        core = lax.axis_index("core")
        mine = lax.dynamic_index_in_dim(packed, core, 1, False)
        send = lax.dynamic_index_in_dim(packed, 1 - core, 1, False)
        return jnp.concatenate([mine, flip(send, "core", 0)], 1)
    got = lax.all_to_all(packed, GROUP, split_axis=1, concat_axis=1, tiled=True)
    return got.reshape(got.shape[0], -1, got.shape[-1])


def to_tokens(values, members):
    count, length, part = values.shape
    tokens = length // members
    if members == 2:
        first = lax.axis_index("core") == 0
        mine = values[:, :tokens]
        other = flip(values[:, tokens:], "core", 0)
        return jnp.where(
            first, jnp.concatenate([mine, other], -1), jnp.concatenate([other, mine], -1)
        )
    got = values.reshape(count, members, tokens, part)
    got = lax.all_to_all(got, GROUP, split_axis=1, concat_axis=1, tiled=True)
    return got.transpose(0, 2, 1, 3).reshape(count, tokens, members * part)


def nt(left, right):
    return lax.dot_general(left, right, (((1,), (1,)), ((), ())), preferred_element_type=F32)


def tn(left, right):
    return lax.dot_general(left, right, (((0,), (0,)), ((), ())), preferred_element_type=F32)


def nn(left, right):
    return jnp.dot(left, right, preferred_element_type=F32)


GROUP = ("xl", "core")


def per_device(
    hidden_in,
    doc_ids,
    w_qkv,
    w_attn_out,
    w_mlp_in,
    w_mlp_out,
    norm_gain_one,
    norm_gain_two,
    out_grad,
):
    parts = lax.axis_size("xg") * lax.axis_size("xl")
    swap = [
        (core * parts + x, (x % 2) * parts + (core * parts + x) // 2)
        for core in range(2)
        for x in range(parts)
    ]
    back = [(there, here) for here, there in swap]
    swapped = ("core", "xg", "xl")
    rows = lax.ppermute(hidden_in[0], swapped, swap)
    ids = lax.ppermute(doc_ids, swapped, swap)[0]
    cotangent = lax.ppermute(out_grad[0], swapped, swap)

    tokens, width = rows.shape
    length = ids.shape[0]
    head_dim = width // HEADS
    member = lax.axis_index("xl") * 2 + lax.axis_index("core")
    plane = lax.axis_index("xg")

    qkv_rows = w_qkv.shape[1]
    out_rows = w_attn_out.shape[1]
    gain_cols = norm_gain_one.shape[0]
    hidden_units = w_mlp_out.shape[0]
    gains = jnp.concatenate([norm_gain_one, norm_gain_two])[None]
    gains = jnp.pad(gains, ((0, 15), (0, width - 2 * gain_cols)))
    mlp_out_t = w_mlp_out.T
    rest = hidden_units - width
    second_shard = jnp.concatenate(
        [w_attn_out.T, w_mlp_in.T, mlp_out_t[:, :width],
         jnp.pad(mlp_out_t[:, width:], ((0, 0), (0, width - rest)))], 0
    )
    first_shard = jnp.concatenate([w_qkv.T, gains], 0)
    bits = bits_of("chip")
    z_first = list(reversed(range(bits)))
    y_first = [0] + z_first[:-1]
    members = parts
    per_member = HEADS // members
    paired = parts == 2

    cut1 = first_shard.shape[0] * 3 // 5 // 16 * 16
    a1 = Lane(first_shard[:cut1], gather_steps(z_first))
    c1 = Lane(first_shard[cut1:], gather_steps(y_first))
    half2 = (second_shard.shape[0] * 5 // 18) // 16 * 16 if paired else 0
    cut2 = second_shard.shape[0] - 2 * half2
    a2 = Lane(second_shard[:cut2], gather_steps(z_first))
    b2 = None
    if half2:
        mine2 = lax.dynamic_slice_in_dim(second_shard, cut2 + plane * half2, half2, 0)
        b2 = Lane(mine2, gather_steps(y_first) + [cross_step()])

    cos_t, sin_t = rope_tables(
        (member * tokens + jnp.arange(tokens)).astype(F32), head_dim, per_member
    )
    places = jnp.arange(length)
    if members == 2:
        places = (places + member * tokens) % length
    cos_h, sin_h = rope_tables(places.astype(F32), head_dim, per_member)
    for phase in range(bits):
        start(a1, c1)
        if phase == 0:
            start(b2)
        elif phase == bits - 1:
            b2.start() if b2 is not None else None
        if phase == 0:
            (rows,) = boundary([a1, c1, b2], rows)
        elif phase == 1:
            cos_t, sin_t, cos_h, sin_h, cotangent = boundary(
                [a1, c1], cos_t, sin_t, cos_h, sin_h, cotangent
            )
        else:
            boundary([a1, c1, b2])
    core1 = [Lane(a1.value, [core_step()]), Lane(c1.value, [core_step()])]
    start(*core1)
    start(b2)
    a2.value = after(a2.value, core1[0].value)
    start(a2)
    boundary(core1)
    fields1 = [(0, qkv_rows), (qkv_rows, gains.shape[0])]
    qkv_full, gain_rows = assemble(
        [(0, core1[0].value[0]), (cut1, core1[1].value[0])],
        [(0, core1[0].value[1]), (cut1, core1[1].value[1])],
        fields1, [width, width],
    )
    gain_rows = gain_rows.reshape(-1, gains.shape[0], width)[:, 0]
    gain_a = gain_rows[:, :gain_cols].reshape(1, width).astype(F32)
    gain_b = gain_rows[:, gain_cols : 2 * gain_cols].reshape(1, width).astype(F32)
    qkv_full, gain_a, gain_b = boundary([a2, b2], qkv_full, gain_a, gain_b)
    start(a2, b2)
    resid = rows.astype(F32)
    packed, h_one = project(rows, gain_a, qkv_full, cos_t, sin_t, members)
    qkv = to_heads(packed)
    if members == 2:
        ids = jnp.where(member == 0, ids, jnp.roll(ids, tokens))
    (qkv,) = boundary([a2], qkv)
    start(a2)
    o_h, lse = attend(qkv, ids, head_dim)
    attn = to_tokens(o_h[None], members)[0]
    (attn,) = boundary([a2, b2], attn)
    drain(a2, b2)
    core2 = [Lane(a2.value, [core_step()])]
    at2 = [0]
    if b2 is not None:
        core2.append(Lane(b2.value, [core_step()]))
        at2.append(cut2)
    start(*core2)
    boundary(core2)
    at = [0, out_rows, out_rows + qkv_rows, 2 * out_rows + qkv_rows]
    attn_full, mlp_in_full, mlp_out_low, mlp_out_high = assemble(
        [(place, lane.value[0]) for place, lane in zip(at2, core2)],
        [(place, lane.value[1]) for place, lane in zip(at2, core2)],
        [(at[0], out_rows), (at[1], qkv_rows), (at[2], out_rows), (at[3], out_rows)],
        [width, width, width, rest],
    )
    mlp_out_full = jnp.concatenate([mlp_out_low, mlp_out_high], -1)
    shards = 2 * lax.axis_size("chip")

    resid_two = resid + nt(attn, attn_full)
    norm_b, inv_b = normalize(resid_two)
    h_two = (norm_b * gain_b).astype(BF16)
    up = nt(h_two, mlp_in_full)
    act_in = up[:, :hidden_units]
    gate_in = up[:, hidden_units:]
    activated = gelu_exact(act_in)
    mixed = (activated * gate_in).astype(BF16)
    result = (resid_two + nt(mixed, mlp_out_full)).astype(BF16)

    cot32 = cotangent.astype(F32)
    g_mlp_out = tn(cotangent, mixed).astype(BF16)
    s_mlp_out = Reduce(
        g_mlp_out.reshape(shards, -1, hidden_units), out_rows // 2 if paired else 0
    )
    start(s_mlp_out.core)
    d_mixed = nn(cotangent, mlp_out_full)
    unused, gelu_back = jax.vjp(gelu_exact, act_in)
    d_act = gelu_back(d_mixed * gate_in)[0]
    d_up = jnp.concatenate([d_act, d_mixed * activated], -1).astype(BF16)
    g_mlp_in = tn(d_up, h_two).astype(BF16)
    s_mlp_in = Reduce(g_mlp_in.reshape(shards, -1, width), pair_rows(qkv_rows))
    ascending = list(range(bits))
    zs_first = ascending[1:] + [0]
    d_up, g_term = boundary([s_mlp_out.core], d_up, s_mlp_in.core.value)
    s_mlp_in.core.value = g_term
    s_mlp_out.open(ascending)
    start(s_mlp_in.core, *s_mlp_out.lanes())
    d_h_two = nn(d_up, mlp_in_full)
    g_gain_b = jnp.sum(d_h_two * norm_b, 0)
    d_resid_two = cot32 + norm_back(d_h_two * gain_b, norm_b, inv_b)
    d_two = d_resid_two.astype(BF16)
    d_attn = nn(d_two, attn_full).astype(BF16)
    d_packed = d_attn.reshape(1, tokens, members, width // members).transpose(0, 2, 1, 3)
    g_attn_out = tn(d_two, attn).astype(BF16)
    s_attn_out = Reduce(g_attn_out.reshape(shards, -1, width), 0)
    d_packed, g_term = boundary([s_mlp_in.core], d_packed, s_attn_out.core.value)
    s_attn_out.core.value = g_term
    s_mlp_in.open(ascending)
    do_h = to_heads(d_packed)[0]
    start(*s_mlp_in.lanes(), s_attn_out.core)
    (do_h,) = boundary([], do_h)
    grads = attend_back(qkv, ids, lse, o_h, do_h, cos_h, sin_h, head_dim)
    moving = s_mlp_in.lanes() + s_mlp_out.lanes()
    (grads,) = boundary(moving + [s_attn_out.core], grads)
    s_attn_out.open(zs_first)
    moving = moving + s_attn_out.lanes()
    returned = to_tokens(grads, members)
    start(*moving)
    d_qkv = jnp.concatenate([returned[0], returned[1], returned[2]], -1)
    g_qkv = tn(d_qkv, h_one).astype(BF16)
    s_qkv = Reduce(g_qkv.reshape(shards, -1, width), pair_rows(qkv_rows))
    d_qkv, g_term, result = boundary(moving, d_qkv, s_qkv.core.value, result)
    s_qkv.core.value = g_term
    start(s_qkv.core, *moving)
    layer_out = lax.ppermute(result, swapped, back)
    d_h_one = nn(d_qkv, qkv_full)
    norm_a, inv_a = normalize(resid)
    g_gain_a = jnp.sum(d_h_one * norm_a, 0)
    input_grad = d_resid_two + norm_back(d_h_one * gain_a, norm_a, inv_a)
    sums = Lane(jnp.stack([g_gain_a, g_gain_b]), total_steps())
    input_grad, totals, layer_out = boundary(
        moving + [s_qkv.core], input_grad.astype(BF16), sums.value, layer_out
    )
    sums.value = totals
    layer_out = layer_out[None]
    s_qkv.open(ascending)
    input_grad = lax.ppermute(input_grad, swapped, back).astype(F32)[None]
    moving = s_qkv.lanes() + moving + [sums]
    drain(*moving)
    gains = sums.value
    offset = (lax.axis_index("chip") * 2 + lax.axis_index("core")) * gain_cols
    gains = lax.dynamic_slice_in_dim(gains, offset, gain_cols, 1)
    return (
        layer_out,
        input_grad,
        s_qkv.close(),
        s_attn_out.close(),
        s_mlp_in.close(),
        s_mlp_out.close(),
        gains[0],
        gains[1],
    )


def solution(mesh):
    fsdp, seq = mesh.shape["fsdp"], mesh.shape["seq"]
    inner = Mesh(
        mesh.devices.reshape(fsdp // 2, 2, 2, seq // 2), ("chip", "core", "xg", "xl")
    )
    rows, parts = ("chip", "core"), ("xg", "xl")
    return jax.shard_map(
        per_device,
        mesh=inner,
        in_specs=(
            P(rows, parts, None),
            P(rows, None),
            P(None, rows),
            P(None, rows),
            P(None, rows),
            P(None, rows),
            P(rows),
            P(rows),
            P(rows, parts, None),
        ),
        out_specs=(
            P(rows, parts, None),
            P(rows, parts, None),
            P(None, rows),
            P(None, rows),
            P(None, rows),
            P(None, rows),
            P(rows),
            P(rows),
        ),
        check_vma=False,
    )
```

```python
import jax
import jax.numpy as jnp
from jax import lax
from jax.experimental import pallas as pl
from jax.experimental.pallas import tpu as pltpu
from jax.sharding import Mesh, PartitionSpec as P

HEADS = 12
rope_base = 160000.0
norm_eps = 1e-05
F32 = jnp.float32
BF16 = jnp.bfloat16


def normalize(values):
    centered = values - jnp.mean(values, -1, keepdims=True)
    inverse = lax.rsqrt(jnp.mean(centered * centered, -1, keepdims=True) + norm_eps)
    return (centered * inverse, inverse)


def norm_back(grad, normed, inverse):
    return inverse * (
        grad
        - jnp.mean(grad, -1, keepdims=True)
        - normed * jnp.mean(grad * normed, -1, keepdims=True)
    )


def gelu_exact(values):
    return jax.nn.gelu(values, approximate=False)


def rope_tables(positions, head_dim, repeats):
    half = head_dim // 2
    inverse = rope_base ** (-(jnp.arange(half).astype(F32) * 2.0 / head_dim))
    angle = positions[:, None] * inverse[None, :]
    repeats = repeats if repeats * head_dim % 128 else 128 // head_dim
    angle = jnp.tile(angle, (1, 2 * repeats))
    return jnp.cos(angle), jnp.sin(angle)


def spread(table, width):
    return jnp.concatenate([table] * (width // table.shape[-1]), -1)


def swap_halves(values, head_dim):
    half = head_dim // 2
    width = values.shape[-1]
    if width % 128 == 0:
        lane = lax.broadcasted_iota(jnp.int32, values.shape, 1)
        low = (lane & (head_dim - 1)) < half
        return jnp.where(
            low, -pltpu.roll(values, width - half, 1), pltpu.roll(values, half, 1)
        )
    pieces = []
    for start in range(0, width, head_dim):
        pieces.append(-values[:, start + half : start + head_dim])
        pieces.append(values[:, start : start + half])
    return jnp.concatenate(pieces, -1)


def vmem_specs(count):
    return [pl.BlockSpec(memory_space=pltpu.VMEM)] * count


PARAMS = dict(vmem_limit_bytes=56 * 1024 * 1024)


def project(rows, gain, weights, cos, sin, members):
    tokens, width = rows.shape
    part = width // members
    head_dim = width // HEADS

    def kernel(rows_ref, gain_ref, w_ref, cos_ref, sin_ref, out_ref, h_ref):
        norm, _ = normalize(rows_ref[...].astype(F32))
        h_ref[...] = (norm * gain_ref[...]).astype(BF16)
        h = h_ref[...]
        cos = spread(cos_ref[...], part)
        sin = spread(sin_ref[...], part)
        for kind in range(3):
            for member in range(members):
                start = kind * width + member * part
                values = lax.dot_general(
                    h, w_ref[start : start + part, :], (((1,), (1,)), ((), ())),
                    preferred_element_type=F32,
                )
                if kind < 2:
                    values = values * cos + swap_halves(values, head_dim) * sin
                out_ref[kind, member] = values.astype(BF16)

    return pl.pallas_call(
        kernel,
        out_shape=(
            jax.ShapeDtypeStruct((3, members, tokens, part), BF16),
            jax.ShapeDtypeStruct((tokens, width), BF16),
        ),
        in_specs=vmem_specs(5),
        out_specs=tuple(vmem_specs(2)),
        compiler_params=pltpu.CompilerParams(**PARAMS),
        name="project",
    )(rows, gain, weights, cos, sin)


def flip(value, axis, bit):
    count = lax.axis_size(axis)
    return lax.ppermute(value, axis, [(i, i ^ (1 << bit)) for i in range(count)])


def bits_of(axis):
    count = lax.axis_size(axis)
    bits = count.bit_length() - 1
    assert count == 1 << bits
    return bits


def after(value, *others):
    return lax.optimization_barrier((value,) + others)[0]


def side(axis, bit=0):
    return (lax.axis_index(axis) >> bit) & 1


def both(value, other, upper, axis):
    upper = upper == 1
    return jnp.stack([jnp.where(upper, other, value), jnp.where(upper, value, other)], axis)


class Lane:
    def __init__(self, value, steps):
        self.value, self.steps, self.pending = value, list(steps), None

    def start(self):
        split, axis, bit, self.join = self.steps.pop(0)
        self.keep, send = split(self.value)
        self.pending = flip(send, axis, bit)

    def finish(self):
        self.value = self.join(self.keep, self.pending)
        self.pending = None


def boundary(lanes, *values):
    lanes = [lane for lane in lanes if lane is not None and lane.pending is not None]
    out = lax.optimization_barrier(tuple(lane.pending for lane in lanes) + tuple(values))
    for lane, got in zip(lanes, out):
        lane.pending = got
        lane.finish()
    return out[len(lanes) :]


def start(*lanes):
    for lane in lanes:
        if lane is not None and lane.steps and lane.pending is None:
            lane.start()


def drain(*lanes):
    while any(lane is not None and lane.steps for lane in lanes):
        start(*lanes)
        boundary(lanes)


def collapse(value):
    return value.reshape((-1,) + value.shape[-2:])


def whole(value):
    return value, value


def gather_steps(order):
    steps, have = [], []
    for bit in order:
        place = sum(other > bit for other in have)
        have.append(bit)
        steps.append(
            (whole, "chip", bit,
             lambda keep, got, bit=bit, place=place: both(keep, got, side("chip", bit), place))
        )
    return steps


def cross_step():
    def join(keep, got):
        pair = both(keep, got, lax.axis_index("xg"), 1)
        return pair.reshape(keep.shape[0], -1, keep.shape[-1])

    return (lambda v: (collapse(v), collapse(v)), "xg", 0, join)


def core_step():
    return (lambda v: (collapse(v), collapse(v)), "core", 0, lambda keep, got: (keep, got))


def add_halves(keep, other):
    return (keep.astype(F32) + other.astype(F32)).astype(BF16)


def halving(axis, bit, place):
    def split(value):
        mine = side(axis, bit)
        return (
            lax.dynamic_index_in_dim(value, mine, place, False),
            lax.dynamic_index_in_dim(value, 1 - mine, place, False),
        )

    return (split, axis, bit, add_halves)


def scatter_steps(order):
    have = list(reversed(range(len(order))))
    steps = []
    for bit in order:
        steps.append(halving("chip", bit, have.index(bit)))
        have.remove(bit)
    return steps


def to_bits(value):
    return value.reshape((2,) * bits_of("chip") + value.shape[-2:])


def sum_steps():
    return [
        (lambda v: whole(v.astype(BF16)), axis, bit,
         lambda keep, got: keep.astype(F32) + got.astype(F32))
        for axis in ("xg", "xl")
        for bit in range(bits_of(axis))
    ]


class Reduce:
    def __init__(self, terms, half):
        self.half = half

        def split(values):
            core = lax.axis_index("core")
            halves = [[], []]
            for value in values:
                pairs = value.reshape((-1, 2) + value.shape[1:])
                for place, which in enumerate((core, 1 - core)):
                    halves[place].append(lax.dynamic_index_in_dim(pairs, which, 1, False))
            return [jnp.concatenate(half, 1) for half in halves]

        self.core = Lane(terms, [(split, "core", 0, add_halves)])
        self.a = self.b = None

    def open(self, order):
        total = self.core.value
        half = self.half
        near = total.shape[1] - 2 * half
        if near:
            self.a = Lane(to_bits(total[:, :near]), scatter_steps(order) + sum_steps())
        if half:
            plane = lax.axis_index("xg")

            def split(value):
                cut = lambda p: lax.dynamic_slice_in_dim(value, near + p * half, half, 1)
                return cut(plane), cut(1 - plane)

            def join(keep, got):
                return to_bits(add_halves(keep, got))

            self.b = Lane(
                total,
                [(split, "xg", 0, join)]
                + scatter_steps(order)
                + [(whole, "xg", 0, lambda keep, got: both(keep, got, lax.axis_index("xg"), 0))],
            )

    def lanes(self):
        return [self.b, self.a]

    def close(self):
        parts = [
            lane.value.reshape((-1,) + lane.value.shape[-1:]).astype(F32)
            for lane in (self.a, self.b)
            if lane is not None
        ]
        return jnp.concatenate(parts, 0)


def pair_rows(rows):
    if lax.axis_size("xg") * lax.axis_size("xl") != 2:
        return 0
    return rows // 4 // 16 * 16


def assemble(sources, fields, shapes):
    core = lax.axis_index("core")
    arrays, copies = [], []
    for start, pair in sources:
        count = pair[0].shape[1]
        for which, array in enumerate(pair):
            arrays.append(array)
            for index in range(array.shape[0]):
                for out, first, rows, columns, column in fields:
                    low, high = max(first, start), min(first + rows, start + count)
                    if low < high:
                        copies.append(
                            (len(arrays) - 1, index, low - start, high - low, out,
                             len(pair), which, rows, low - first, columns, column)
                        )

    def kernel(core_ref, *refs):
        ins, outs = refs[: len(arrays)], refs[len(arrays) : -1]
        sems = refs[-1]
        started = []
        for number, copy in enumerate(copies):
            source, index, low, size, out, pairs, which, rows, offset, columns, column = copy
            at = index
            if pairs == 2:
                at = 2 * index + (core_ref[0] if which == 0 else 1 - core_ref[0])
            base = at * rows + offset
            if pairs == 2:
                base = pl.multiple_of(base, 16)
            handle = pltpu.make_async_copy(
                ins[source].at[index, low : low + size, :columns],
                outs[out].at[pl.ds(base, size), column : column + columns],
                sems.at[number],
            )
            handle.start()
            started.append(handle)
        for handle in started:
            handle.wait()

    return pl.pallas_call(
        kernel,
        out_shape=tuple(jax.ShapeDtypeStruct(shape, BF16) for shape in shapes),
        in_specs=[pl.BlockSpec(memory_space=pltpu.SMEM)]
        + [pl.BlockSpec(memory_space=pl.ANY)] * len(arrays),
        out_specs=tuple(vmem_specs(len(shapes))),
        scratch_shapes=[pltpu.SemaphoreType.DMA((len(copies),))],
        compiler_params=pltpu.CompilerParams(**PARAMS),
        name="assemble",
    )(core[None].astype(jnp.int32), *arrays)


def total_steps():
    return [
        (whole, axis, bit, lambda keep, got: keep + got)
        for axis in ("core", "chip", "xg", "xl")
        for bit in range(bits_of(axis))
    ]


def attend(qkv, ids, head_dim):
    length, part = qkv.shape[1:]
    heads = part // head_dim
    scale = head_dim ** (-0.5)

    def kernel(qkv_ref, row_ref, col_ref, out_ref, lse_ref):
        keep = col_ref[...] == row_ref[...]
        for head in range(heads):
            lanes = slice(head * head_dim, (head + 1) * head_dim)
            scores = lax.dot_general(
                qkv_ref[0, :, lanes], qkv_ref[1, :, lanes], (((1,), (1,)), ((), ())),
                preferred_element_type=F32,
            ) * scale
            scores = jnp.where(keep, scores, -jnp.inf)
            top = jnp.max(scores, -1, keepdims=True)
            weight = jnp.exp(scores - top)
            total = jnp.sum(weight, -1, keepdims=True)
            out = jnp.dot(weight.astype(BF16), qkv_ref[2, :, lanes], preferred_element_type=F32)
            out_ref[:, lanes] = (out / total).astype(BF16)
            lse_ref[:, head : head + 1] = top + jnp.log(total)

    return pl.pallas_call(
        kernel,
        out_shape=(
            jax.ShapeDtypeStruct((length, part), BF16),
            jax.ShapeDtypeStruct((length, heads), F32),
        ),
        in_specs=vmem_specs(3),
        out_specs=tuple(vmem_specs(2)),
        compiler_params=pltpu.CompilerParams(**PARAMS),
        name="attend",
    )(qkv, ids[None, :], ids[:, None])


def attend_back(qkv, ids, lse, out, d_out, cos, sin, head_dim):
    length, part = qkv.shape[1:]
    heads = part // head_dim
    scale = head_dim ** (-0.5)

    def kernel(qkv_ref, row_ref, col_ref, lse_ref, out_ref, do_ref, cos_ref, sin_ref, grad_ref, dq_ref, dk_ref):
        keep = col_ref[...] == row_ref[...]
        for head in range(heads):
            lanes = slice(head * head_dim, (head + 1) * head_dim)
            query = qkv_ref[0, :, lanes]
            key = qkv_ref[1, :, lanes]
            d_head = do_ref[:, lanes]
            scores = lax.dot_general(
                query, key, (((1,), (1,)), ((), ())), preferred_element_type=F32
            ) * scale
            prob = jnp.where(keep, jnp.exp(scores - lse_ref[:, head : head + 1]), 0.0)
            d_prob = lax.dot_general(
                d_head, qkv_ref[2, :, lanes], (((1,), (1,)), ((), ())),
                preferred_element_type=F32,
            )
            delta = jnp.sum(d_head.astype(F32) * out_ref[:, lanes].astype(F32), -1, keepdims=True)
            d_score = (prob * (d_prob - delta)).astype(BF16)
            grad_ref[2, :, lanes] = lax.dot_general(
                prob.astype(BF16), d_head, (((0,), (0,)), ((), ())), preferred_element_type=F32
            ).astype(BF16)
            dq_ref[:, lanes] = jnp.dot(d_score, key, preferred_element_type=F32) * scale
            dk_ref[:, lanes] = lax.dot_general(
                d_score, query, (((0,), (0,)), ((), ())), preferred_element_type=F32
            ) * scale
        for kind, ref in enumerate((dq_ref, dk_ref)):
            values = ref[...]
            cos = spread(cos_ref[...], part)
            sin = spread(sin_ref[...], part)
            turned = values * cos - swap_halves(values * sin, head_dim)
            grad_ref[kind] = turned.astype(BF16)

    return pl.pallas_call(
        kernel,
        out_shape=jax.ShapeDtypeStruct((3, length, part), BF16),
        in_specs=vmem_specs(8),
        out_specs=vmem_specs(1)[0],
        scratch_shapes=[pltpu.VMEM((length, part), F32)] * 2,
        compiler_params=pltpu.CompilerParams(**PARAMS),
        name="attend_back",
    )(qkv, ids[None, :], ids[:, None], lse, out, d_out, cos, sin)


def to_heads(packed):
    members = packed.shape[1]
    if members == 2:
        core = lax.axis_index("core")
        mine = lax.dynamic_index_in_dim(packed, core, 1, False)
        send = lax.dynamic_index_in_dim(packed, 1 - core, 1, False)
        return jnp.concatenate([mine, flip(send, "core", 0)], 1)
    got = lax.all_to_all(packed, GROUP, split_axis=1, concat_axis=1, tiled=True)
    return got.reshape(got.shape[0], -1, got.shape[-1])


def to_tokens(values, members):
    count, length, part = values.shape
    tokens = length // members
    if members == 2:
        first = lax.axis_index("core") == 0
        mine = values[:, :tokens]
        other = flip(values[:, tokens:], "core", 0)
        return jnp.where(
            first, jnp.concatenate([mine, other], -1), jnp.concatenate([other, mine], -1)
        )
    got = values.reshape(count, members, tokens, part)
    got = lax.all_to_all(got, GROUP, split_axis=1, concat_axis=1, tiled=True)
    return got.transpose(0, 2, 1, 3).reshape(count, tokens, members * part)


def nt(left, right):
    return lax.dot_general(left, right, (((1,), (1,)), ((), ())), preferred_element_type=F32)


def tn(left, right):
    return lax.dot_general(left, right, (((0,), (0,)), ((), ())), preferred_element_type=F32)


def nn(left, right):
    return jnp.dot(left, right, preferred_element_type=F32)


GROUP = ("xl", "core")


def per_device(
    hidden_in,
    doc_ids,
    w_qkv,
    w_attn_out,
    w_mlp_in,
    w_mlp_out,
    norm_gain_one,
    norm_gain_two,
    out_grad,
):
    parts = lax.axis_size("xg") * lax.axis_size("xl")
    swap = [
        (core * parts + x, (x % 2) * parts + (core * parts + x) // 2)
        for core in range(2)
        for x in range(parts)
    ]
    back = [(there, here) for here, there in swap]
    swapped = ("core", "xg", "xl")
    tokens, width = hidden_in.shape[1:]
    length = doc_ids.shape[1]
    id_row = jnp.pad(doc_ids.astype(BF16), ((0, 15), (0, width - length)))
    bundle = lax.ppermute(
        jnp.concatenate([hidden_in[0], out_grad[0], id_row], 0), swapped, swap
    )
    head_dim = width // HEADS
    member = lax.axis_index("xl") * 2 + lax.axis_index("core")
    plane = lax.axis_index("xg")

    qkv_rows = w_qkv.shape[1]
    out_rows = w_attn_out.shape[1]
    gain_cols = norm_gain_one.shape[0]
    hidden_units = w_mlp_out.shape[0]
    gains = jnp.concatenate([norm_gain_one, norm_gain_two])[None]
    gains = jnp.pad(gains, ((0, 15), (0, width - 2 * gain_cols)))
    mlp_out_t = w_mlp_out.T
    rest = hidden_units - width
    second_shard = jnp.concatenate(
        [w_attn_out.T, w_mlp_in.T, mlp_out_t[:, :width],
         jnp.pad(mlp_out_t[:, width:], ((0, 0), (0, width - rest)))], 0
    )
    second = lax.all_gather(second_shard, ("chip", "core"), axis=0, tiled=False)
    first_shard = jnp.concatenate([w_qkv.T, gains], 0)
    bits = bits_of("chip")
    z_first = list(reversed(range(bits)))
    y_first = [0] + z_first[:-1]
    members = parts
    per_member = HEADS // members
    paired = parts == 2

    cut1 = first_shard.shape[0] * 3 // 5 // 16 * 16
    a1 = Lane(first_shard[:cut1], gather_steps(z_first))
    c1 = Lane(first_shard[cut1:], gather_steps(y_first))
    cos_t, sin_t = rope_tables(
        (member * tokens + jnp.arange(tokens)).astype(F32), head_dim, per_member
    )
    places = jnp.arange(length)
    if members == 2:
        places = (places + member * tokens) % length
    cos_h, sin_h = rope_tables(places.astype(F32), head_dim, per_member)
    for phase in range(bits):
        start(a1, c1)
        if phase == 0:
            boundary([a1, c1])
        elif phase == 1:
            cos_t, sin_t, cos_h, sin_h, bundle = boundary(
                [a1, c1], cos_t, sin_t, cos_h, sin_h, bundle
            )
        else:
            boundary([a1, c1])
    rows, cotangent = bundle[:tokens], bundle[tokens : 2 * tokens]
    ids = bundle[2 * tokens, :length].astype(jnp.int32)
    core1 = [Lane(a1.value, [core_step()]), Lane(c1.value, [core_step()])]
    start(*core1)
    boundary(core1)
    aligned = qkv_rows % 16 == 0 and out_rows % 16 == 0
    count = 2 * lax.axis_size("chip")
    pad_rows = gains.shape[0]
    if aligned:
        qkv_full, gain_rows = assemble(
            [(0, core1[0].value), (cut1, core1[1].value)],
            [(0, 0, qkv_rows, width, 0), (1, qkv_rows, pad_rows, width, 0)],
            [(count * qkv_rows, width), (count * pad_rows, width)],
        )
    else:
        core = lax.axis_index("core")
        mixed_rows = jnp.concatenate(
            [collapse(both(*lane.value, core, 1)) for lane in core1], 1
        )
        qkv_full = mixed_rows[:, :qkv_rows].reshape(-1, width)
        gain_rows = mixed_rows[:, qkv_rows:]
    gain_rows = gain_rows.reshape(-1, gains.shape[0], width)[:, 0]
    gain_a = gain_rows[:, :gain_cols].reshape(1, width).astype(F32)
    gain_b = gain_rows[:, gain_cols : 2 * gain_cols].reshape(1, width).astype(F32)
    resid = rows.astype(F32)
    packed, h_one = project(rows, gain_a, qkv_full, cos_t, sin_t, members)
    qkv = to_heads(packed)
    if members == 2:
        ids = jnp.where(member == 0, ids, jnp.roll(ids, tokens))
    o_h, lse = attend(qkv, ids, head_dim)
    attn = to_tokens(o_h[None], members)[0]
    (attn, second) = boundary([], attn, second)
    at = [0, out_rows, out_rows + qkv_rows, 2 * out_rows + qkv_rows]
    if aligned and rest % 128 == 0:
        attn_full, mlp_in_full, mlp_out_full = assemble(
            [(0, [second])],
            [
                (0, at[0], out_rows, width, 0),
                (1, at[1], qkv_rows, width, 0),
                (2, at[2], out_rows, width, 0),
                (2, at[3], out_rows, rest, width),
            ],
            [(width, width), (count * qkv_rows, width), (width, hidden_units)],
        )
    else:
        attn_full = second[:, : at[1]].reshape(-1, width)
        mlp_in_full = second[:, at[1] : at[2]].reshape(-1, width)
        mlp_out_full = jnp.concatenate(
            [second[:, at[2] : at[3]], second[:, at[3] :, :rest]], -1
        ).reshape(width, hidden_units)

    resid_two = resid + nt(attn, attn_full)
    norm_b, inv_b = normalize(resid_two)
    h_two = (norm_b * gain_b).astype(BF16)
    up = nt(h_two, mlp_in_full)
    act_in = up[:, :hidden_units]
    gate_in = up[:, hidden_units:]
    activated = gelu_exact(act_in)
    mixed = (activated * gate_in).astype(BF16)
    result = (resid_two + nt(mixed, mlp_out_full)).astype(BF16)

    cot32 = cotangent.astype(F32)
    g_mlp_low = tn(cotangent, mixed[:, :width]).astype(BF16)
    g_mlp_high = tn(cotangent, mixed[:, width:]).astype(BF16)
    d_mixed = nn(cotangent, mlp_out_full)
    unused, gelu_back = jax.vjp(gelu_exact, act_in)
    d_act = gelu_back(d_mixed * gate_in)[0]
    d_up = jnp.concatenate([d_act, d_mixed * activated], -1).astype(BF16)
    g_mlp_in = tn(d_up, h_two).astype(BF16)
    ascending = list(range(bits))
    d_h_two = nn(d_up, mlp_in_full)
    g_gain_b = jnp.sum(d_h_two * norm_b, 0)
    d_resid_two = cot32 + norm_back(d_h_two * gain_b, norm_b, inv_b)
    d_two = d_resid_two.astype(BF16)
    d_attn = nn(d_two, attn_full).astype(BF16)
    d_packed = d_attn.reshape(1, tokens, members, width // members).transpose(0, 2, 1, 3)
    g_attn_out = tn(d_two, attn).astype(BF16)

    spare = jnp.pad(
        g_gain_b.astype(BF16).reshape(count, 1, gain_cols),
        ((0, 0), (0, out_rows - 1), (0, width - rest - gain_cols)),
    )
    terms = [
        g_attn_out.reshape(count, -1, width),
        g_mlp_in.reshape(count, -1, width),
        g_mlp_low.reshape(count, -1, width),
        jnp.concatenate([g_mlp_high.reshape(count, -1, rest), spare], -1),
    ]
    d_packed, *terms = boundary([], d_packed, *terms)
    s_mlp = Reduce(terms, pair_rows(at[3] + out_rows))
    start(s_mlp.core)
    do_h = to_heads(d_packed)[0]
    (do_h,) = boundary([s_mlp.core], do_h)
    s_mlp.open(ascending)
    start(*s_mlp.lanes())
    (do_h,) = boundary([], do_h)
    grads = attend_back(qkv, ids, lse, o_h, do_h, cos_h, sin_h, head_dim)
    moving = s_mlp.lanes()
    returned = to_tokens(grads, members)
    d_qkv = jnp.concatenate([returned[0], returned[1], returned[2]], -1)
    g_qkv = tn(d_qkv, h_one).astype(BF16)
    s_qkv = Reduce([g_qkv.reshape(count, -1, width)], pair_rows(qkv_rows))
    d_qkv, g_term, result = boundary(moving, d_qkv, s_qkv.core.value[0], result)
    s_qkv.core.value = [g_term]
    start(s_qkv.core, *moving)
    layer_out = lax.ppermute(result, swapped, back)
    d_h_one = nn(d_qkv, qkv_full)
    norm_a, inv_a = normalize(resid)
    g_gain_a = jnp.sum(d_h_one * norm_a, 0)
    input_grad = d_resid_two + norm_back(d_h_one * gain_a, norm_a, inv_a)
    sums = Lane(g_gain_a[None], total_steps())
    input_grad, totals, layer_out = boundary(
        moving + [s_qkv.core], input_grad.astype(BF16), sums.value, layer_out
    )
    sums.value = totals
    layer_out = layer_out[None]
    s_qkv.open(ascending)
    input_grad = lax.ppermute(input_grad, swapped, back).astype(F32)[None]
    moving = s_qkv.lanes() + moving + [sums]
    drain(*moving)
    gains = sums.value
    offset = (lax.axis_index("chip") * 2 + lax.axis_index("core")) * gain_cols
    gains = lax.dynamic_slice_in_dim(gains, offset, gain_cols, 1)
    summed = s_mlp.close()
    return (
        layer_out,
        input_grad,
        s_qkv.close().T,
        summed[: at[1]].T,
        summed[at[1] : at[2]].T,
        jnp.concatenate([summed[at[2] : at[3]], summed[at[3] :, :rest]], -1).T,
        gains[0],
        summed[at[3], rest : rest + gain_cols],
    )


def solution(mesh):
    fsdp, seq = mesh.shape["fsdp"], mesh.shape["seq"]
    inner = Mesh(
        mesh.devices.reshape(fsdp // 2, 2, 2, seq // 2), ("chip", "core", "xg", "xl")
    )
    rows, parts = ("chip", "core"), ("xg", "xl")
    return jax.shard_map(
        per_device,
        mesh=inner,
        in_specs=(
            P(rows, parts, None),
            P(rows, None),
            P(None, rows),
            P(None, rows),
            P(None, rows),
            P(None, rows),
            P(rows),
            P(rows),
            P(rows, parts, None),
        ),
        out_specs=(
            P(rows, parts, None),
            P(rows, parts, None),
            P(None, rows),
            P(None, rows),
            P(None, rows),
            P(None, rows),
            P(rows),
            P(rows),
        ),
        check_vma=False,
    )
```

```python
import jax
import jax.numpy as jnp
from jax import lax
from jax.experimental import pallas as pl
from jax.experimental.pallas import tpu as pltpu
from jax.sharding import Mesh, PartitionSpec as P

HEADS = 12
rope_base = 160000.0
norm_eps = 1e-05
F32 = jnp.float32
BF16 = jnp.bfloat16


def normalize(values):
    centered = values - jnp.mean(values, -1, keepdims=True)
    inverse = lax.rsqrt(jnp.mean(centered * centered, -1, keepdims=True) + norm_eps)
    return (centered * inverse, inverse)


def norm_back(grad, normed, inverse):
    return inverse * (
        grad
        - jnp.mean(grad, -1, keepdims=True)
        - normed * jnp.mean(grad * normed, -1, keepdims=True)
    )


def gelu_exact(values):
    return jax.nn.gelu(values, approximate=False)


def rope_tables(positions, head_dim, repeats):
    half = head_dim // 2
    inverse = rope_base ** (-(jnp.arange(half).astype(F32) * 2.0 / head_dim))
    angle = positions[:, None] * inverse[None, :]
    repeats = repeats if repeats * head_dim % 128 else 128 // head_dim
    angle = jnp.tile(angle, (1, 2 * repeats))
    return jnp.cos(angle), jnp.sin(angle)


def spread(table, width):
    return jnp.concatenate([table] * (width // table.shape[-1]), -1)


def swap_halves(values, head_dim):
    half = head_dim // 2
    width = values.shape[-1]
    if width % 128 == 0:
        lane = lax.broadcasted_iota(jnp.int32, values.shape, 1)
        low = (lane & (head_dim - 1)) < half
        return jnp.where(
            low, -pltpu.roll(values, width - half, 1), pltpu.roll(values, half, 1)
        )
    pieces = []
    for start in range(0, width, head_dim):
        pieces.append(-values[:, start + half : start + head_dim])
        pieces.append(values[:, start : start + half])
    return jnp.concatenate(pieces, -1)


def vmem_specs(count):
    return [pl.BlockSpec(memory_space=pltpu.VMEM)] * count


PARAMS = dict(vmem_limit_bytes=56 * 1024 * 1024)


def project(rows, gain, weights, cos, sin, members):
    tokens, width = rows.shape
    part = width // members
    head_dim = width // HEADS

    def kernel(rows_ref, gain_ref, w_ref, cos_ref, sin_ref, out_ref, h_ref):
        norm, _ = normalize(rows_ref[...].astype(F32))
        h_ref[...] = (norm * gain_ref[...]).astype(BF16)
        h = h_ref[...]
        cos = spread(cos_ref[...], part)
        sin = spread(sin_ref[...], part)
        for kind in range(3):
            for member in range(members):
                start = kind * width + member * part
                values = lax.dot_general(
                    h, w_ref[start : start + part, :], (((1,), (1,)), ((), ())),
                    preferred_element_type=F32,
                )
                if kind < 2:
                    values = values * cos + swap_halves(values, head_dim) * sin
                out_ref[kind, member] = values.astype(BF16)

    return pl.pallas_call(
        kernel,
        out_shape=(
            jax.ShapeDtypeStruct((3, members, tokens, part), BF16),
            jax.ShapeDtypeStruct((tokens, width), BF16),
        ),
        in_specs=vmem_specs(5),
        out_specs=tuple(vmem_specs(2)),
        compiler_params=pltpu.CompilerParams(**PARAMS),
        name="project",
    )(rows, gain, weights, cos, sin)


def flip(value, axis, bit):
    count = lax.axis_size(axis)
    return lax.ppermute(value, axis, [(i, i ^ (1 << bit)) for i in range(count)])


def bits_of(axis):
    count = lax.axis_size(axis)
    bits = count.bit_length() - 1
    assert count == 1 << bits
    return bits


def after(value, *others):
    return lax.optimization_barrier((value,) + others)[0]


def side(axis, bit=0):
    return (lax.axis_index(axis) >> bit) & 1


def both(value, other, upper, axis):
    upper = upper == 1
    return jnp.stack([jnp.where(upper, other, value), jnp.where(upper, value, other)], axis)


class Lane:
    def __init__(self, value, steps):
        self.value, self.steps, self.pending = value, list(steps), None

    def prepare(self):
        split, self.axis, self.bit, self.join = self.steps.pop(0)
        self.keep, self.sending = split(self.value)

    def launch(self):
        self.pending = flip(self.sending, self.axis, self.bit)

    def start(self):
        self.prepare()
        self.launch()

    def finish(self):
        self.value = self.join(self.keep, self.pending)
        self.pending = None


def boundary(lanes, *values):
    lanes = [lane for lane in lanes if lane is not None and lane.pending is not None]
    out = lax.optimization_barrier(tuple(lane.pending for lane in lanes) + tuple(values))
    for lane, got in zip(lanes, out):
        lane.pending = got
        lane.finish()
    return out[len(lanes) :]


def start(*lanes):
    for lane in lanes:
        if lane is not None and lane.steps and lane.pending is None:
            lane.start()


def start_with(lanes, *values):
    lanes = [lane for lane in lanes if lane is not None and lane.steps and lane.pending is None]
    for lane in lanes:
        lane.prepare()
    out = lax.optimization_barrier(tuple(lane.sending for lane in lanes) + tuple(values))
    for lane, send in zip(lanes, out):
        lane.sending = send
        lane.launch()
    return out[len(lanes) :]


def drain(*lanes):
    while any(lane is not None and lane.steps for lane in lanes):
        start(*lanes)
        boundary(lanes)


def collapse(value):
    return value.reshape((-1,) + value.shape[-2:])


def whole(value):
    return value, value


def gather_steps(order):
    steps, have = [], []
    for bit in order:
        place = sum(other > bit for other in have)
        have.append(bit)
        steps.append(
            (whole, "chip", bit,
             lambda keep, got, bit=bit, place=place: both(keep, got, side("chip", bit), place))
        )
    return steps


def cross_step():
    def join(keep, got):
        pair = both(keep, got, lax.axis_index("xg"), 1)
        return pair.reshape(keep.shape[0], -1, keep.shape[-1])

    return (lambda v: (collapse(v), collapse(v)), "xg", 0, join)


def core_step():
    return (lambda v: (collapse(v), collapse(v)), "core", 0, lambda keep, got: (keep, got))


def add_halves(keep, other):
    return (keep.astype(F32) + other.astype(F32)).astype(BF16)


def halving(axis, bit, place):
    def split(value):
        mine = side(axis, bit)
        return (
            lax.dynamic_index_in_dim(value, mine, place, False),
            lax.dynamic_index_in_dim(value, 1 - mine, place, False),
        )

    return (split, axis, bit, add_halves)


def scatter_steps(order):
    have = list(reversed(range(len(order))))
    steps = []
    for bit in order:
        steps.append(halving("chip", bit, have.index(bit)))
        have.remove(bit)
    return steps


def to_bits(value):
    return value.reshape((2,) * bits_of("chip") + value.shape[-2:])


def sum_steps():
    return [
        (lambda v: whole(v.astype(BF16)), axis, bit,
         lambda keep, got: keep.astype(F32) + got.astype(F32))
        for axis in ("xg", "xl")
        for bit in range(bits_of(axis))
    ]


class Reduce:
    def __init__(self, term, half):
        self.half = half

        pairs = term.reshape((-1, 2) + term.shape[1:])
        self.core = Lane(pairs, [halving("core", 0, 1)])
        self.a = self.b = None

    def open(self, order):
        total = self.core.value
        half = self.half
        near = total.shape[1] - 2 * half
        if near:
            self.a = Lane(to_bits(total[:, :near]), scatter_steps(order) + sum_steps())
        if half:
            plane = lax.axis_index("xg")

            def split(value):
                cut = lambda p: lax.dynamic_slice_in_dim(value, near + p * half, half, 1)
                return cut(plane), cut(1 - plane)

            def join(keep, got):
                return to_bits(add_halves(keep, got))

            self.b = Lane(
                total,
                [(split, "xg", 0, join)]
                + scatter_steps(order)
                + [(whole, "xg", 0, lambda keep, got: both(keep, got, lax.axis_index("xg"), 0))],
            )

    def lanes(self):
        return [self.b, self.a]

    def close(self):
        parts = [
            lane.value.reshape((-1,) + lane.value.shape[-1:]).astype(F32)
            for lane in (self.a, self.b)
            if lane is not None
        ]
        return jnp.concatenate(parts, 0).T


def pair_rows(rows):
    if lax.axis_size("xg") * lax.axis_size("xl") != 2:
        return 0
    return rows // 4 // 16 * 16


def assemble(sources, fields, shapes):
    core = lax.axis_index("core")
    arrays, copies = [], []
    for start, pair in sources:
        count = pair[0].shape[1]
        for which, array in enumerate(pair):
            arrays.append(array)
            for index in range(array.shape[0]):
                for out, first, rows, columns, column in fields:
                    low, high = max(first, start), min(first + rows, start + count)
                    if low < high:
                        copies.append(
                            (len(arrays) - 1, index, low - start, high - low, out,
                             len(pair), which, rows, low - first, columns, column)
                        )

    def kernel(core_ref, *refs):
        ins, outs = refs[: len(arrays)], refs[len(arrays) : -1]
        sems = refs[-1]
        started = []
        for number, copy in enumerate(copies):
            source, index, low, size, out, pairs, which, rows, offset, columns, column = copy
            at = index
            if pairs == 2:
                at = 2 * index + (core_ref[0] if which == 0 else 1 - core_ref[0])
            base = at * rows + offset
            if pairs == 2:
                base = pl.multiple_of(base, 16)
            handle = pltpu.make_async_copy(
                ins[source].at[index, low : low + size, :columns],
                outs[out].at[pl.ds(base, size), column : column + columns],
                sems.at[number],
            )
            handle.start()
            started.append(handle)
        for handle in started:
            handle.wait()

    return pl.pallas_call(
        kernel,
        out_shape=tuple(jax.ShapeDtypeStruct(shape, BF16) for shape in shapes),
        in_specs=[pl.BlockSpec(memory_space=pltpu.SMEM)]
        + [pl.BlockSpec(memory_space=pl.ANY)] * len(arrays),
        out_specs=tuple(vmem_specs(len(shapes))),
        scratch_shapes=[pltpu.SemaphoreType.DMA((len(copies),))],
        compiler_params=pltpu.CompilerParams(**PARAMS),
        name="assemble",
    )(core[None].astype(jnp.int32), *arrays)


def total_steps():
    return [
        (whole, axis, bit, lambda keep, got: keep + got)
        for axis in ("core", "chip", "xg", "xl")
        for bit in range(bits_of(axis))
    ]


def attend(qkv, ids, head_dim):
    length, part = qkv.shape[1:]
    heads = part // head_dim
    scale = head_dim ** (-0.5)

    def kernel(qkv_ref, row_ref, col_ref, out_ref, lse_ref):
        keep = col_ref[...] == row_ref[...]
        for head in range(heads):
            lanes = slice(head * head_dim, (head + 1) * head_dim)
            scores = lax.dot_general(
                qkv_ref[0, :, lanes], qkv_ref[1, :, lanes], (((1,), (1,)), ((), ())),
                preferred_element_type=F32,
            ) * scale
            scores = jnp.where(keep, scores, -jnp.inf)
            top = jnp.max(scores, -1, keepdims=True)
            weight = jnp.exp(scores - top)
            total = jnp.sum(weight, -1, keepdims=True)
            out = jnp.dot(weight.astype(BF16), qkv_ref[2, :, lanes], preferred_element_type=F32)
            out_ref[:, lanes] = (out / total).astype(BF16)
            lse_ref[:, head : head + 1] = top + jnp.log(total)

    return pl.pallas_call(
        kernel,
        out_shape=(
            jax.ShapeDtypeStruct((length, part), BF16),
            jax.ShapeDtypeStruct((length, heads), F32),
        ),
        in_specs=vmem_specs(3),
        out_specs=tuple(vmem_specs(2)),
        compiler_params=pltpu.CompilerParams(**PARAMS),
        name="attend",
    )(qkv, ids[None, :], ids[:, None])


def attend_back(qkv, ids, lse, out, d_out, cos, sin, head_dim):
    length, part = qkv.shape[1:]
    heads = part // head_dim
    scale = head_dim ** (-0.5)

    def kernel(qkv_ref, row_ref, col_ref, lse_ref, out_ref, do_ref, cos_ref, sin_ref, grad_ref, dq_ref, dk_ref):
        keep = col_ref[...] == row_ref[...]
        for head in range(heads):
            lanes = slice(head * head_dim, (head + 1) * head_dim)
            query = qkv_ref[0, :, lanes]
            key = qkv_ref[1, :, lanes]
            d_head = do_ref[:, lanes]
            scores = lax.dot_general(
                query, key, (((1,), (1,)), ((), ())), preferred_element_type=F32
            ) * scale
            prob = jnp.where(keep, jnp.exp(scores - lse_ref[:, head : head + 1]), 0.0)
            d_prob = lax.dot_general(
                d_head, qkv_ref[2, :, lanes], (((1,), (1,)), ((), ())),
                preferred_element_type=F32,
            )
            delta = jnp.sum(d_head.astype(F32) * out_ref[:, lanes].astype(F32), -1, keepdims=True)
            d_score = (prob * (d_prob - delta)).astype(BF16)
            grad_ref[2, :, lanes] = lax.dot_general(
                prob.astype(BF16), d_head, (((0,), (0,)), ((), ())), preferred_element_type=F32
            ).astype(BF16)
            dq_ref[:, lanes] = jnp.dot(d_score, key, preferred_element_type=F32) * scale
            dk_ref[:, lanes] = lax.dot_general(
                d_score, query, (((0,), (0,)), ((), ())), preferred_element_type=F32
            ) * scale
        for kind, ref in enumerate((dq_ref, dk_ref)):
            values = ref[...]
            cos = spread(cos_ref[...], part)
            sin = spread(sin_ref[...], part)
            turned = values * cos - swap_halves(values * sin, head_dim)
            grad_ref[kind] = turned.astype(BF16)

    return pl.pallas_call(
        kernel,
        out_shape=jax.ShapeDtypeStruct((3, length, part), BF16),
        in_specs=vmem_specs(8),
        out_specs=vmem_specs(1)[0],
        scratch_shapes=[pltpu.VMEM((length, part), F32)] * 2,
        compiler_params=pltpu.CompilerParams(**PARAMS),
        name="attend_back",
    )(qkv, ids[None, :], ids[:, None], lse, out, d_out, cos, sin)


def to_heads(packed):
    members = packed.shape[1]
    if members == 2:
        core = lax.axis_index("core")
        mine = lax.dynamic_index_in_dim(packed, core, 1, False)
        send = lax.dynamic_index_in_dim(packed, 1 - core, 1, False)
        return jnp.concatenate([mine, flip(send, "core", 0)], 1)
    got = lax.all_to_all(packed, GROUP, split_axis=1, concat_axis=1, tiled=True)
    return got.reshape(got.shape[0], -1, got.shape[-1])


def to_tokens(values, members):
    count, length, part = values.shape
    tokens = length // members
    if members == 2:
        first = lax.axis_index("core") == 0
        mine = values[:, :tokens]
        other = flip(values[:, tokens:], "core", 0)
        return jnp.where(
            first, jnp.concatenate([mine, other], -1), jnp.concatenate([other, mine], -1)
        )
    got = values.reshape(count, members, tokens, part)
    got = lax.all_to_all(got, GROUP, split_axis=1, concat_axis=1, tiled=True)
    return got.transpose(0, 2, 1, 3).reshape(count, tokens, members * part)


def nt(left, right):
    return lax.dot_general(left, right, (((1,), (1,)), ((), ())), preferred_element_type=F32)


def tn(left, right):
    return lax.dot_general(left, right, (((0,), (0,)), ((), ())), preferred_element_type=F32)


def nn(left, right):
    return jnp.dot(left, right, preferred_element_type=F32)


GROUP = ("xl", "core")


def per_device(
    hidden_in,
    doc_ids,
    w_qkv,
    w_attn_out,
    w_mlp_in,
    w_mlp_out,
    norm_gain_one,
    norm_gain_two,
    out_grad,
):
    parts = lax.axis_size("xg") * lax.axis_size("xl")
    swap = [
        (core * parts + x, (x % 2) * parts + (core * parts + x) // 2)
        for core in range(2)
        for x in range(parts)
    ]
    back = [(there, here) for here, there in swap]
    swapped = ("core", "xg", "xl")
    tokens, width = hidden_in.shape[1:]
    length = doc_ids.shape[1]
    id_row = jnp.pad(doc_ids.astype(BF16), ((0, 15), (0, width - length)))
    bundle = lax.ppermute(
        jnp.concatenate([hidden_in[0], out_grad[0], id_row], 0), swapped, swap
    )
    head_dim = width // HEADS
    member = lax.axis_index("xl") * 2 + lax.axis_index("core")
    plane = lax.axis_index("xg")

    qkv_rows = w_qkv.shape[1]
    out_rows = w_attn_out.shape[1]
    gain_cols = norm_gain_one.shape[0]
    hidden_units = w_mlp_out.shape[0]
    gains = jnp.concatenate([norm_gain_one, norm_gain_two])[None]
    gains = jnp.pad(gains, ((0, 15), (0, width - 2 * gain_cols)))
    mlp_out_t = w_mlp_out.T
    rest = hidden_units - width
    second_shard = jnp.concatenate(
        [w_attn_out.T, w_mlp_in.T, mlp_out_t[:, :width],
         jnp.pad(mlp_out_t[:, width:], ((0, 0), (0, width - rest)))], 0
    )
    second = lax.all_gather(second_shard, ("chip", "core"), axis=0, tiled=False)
    first_shard = jnp.concatenate([w_qkv.T, gains], 0)
    bits = bits_of("chip")
    z_first = list(reversed(range(bits)))
    y_first = [0] + z_first[:-1]
    members = parts
    per_member = HEADS // members
    paired = parts == 2

    cut1 = first_shard.shape[0] * 3 // 5 // 16 * 16
    a1 = Lane(first_shard[:cut1], gather_steps(z_first))
    c1 = Lane(first_shard[cut1:], gather_steps(y_first))
    cos_t, sin_t = rope_tables(
        (member * tokens + jnp.arange(tokens)).astype(F32), head_dim, per_member
    )
    places = jnp.arange(length)
    if members == 2:
        places = (places + member * tokens) % length
    cos_h, sin_h = rope_tables(places.astype(F32), head_dim, per_member)
    for phase in range(bits):
        start(a1, c1)
        if phase == 0:
            boundary([a1, c1])
        elif phase == 1:
            cos_t, sin_t, cos_h, sin_h, bundle = boundary(
                [a1, c1], cos_t, sin_t, cos_h, sin_h, bundle
            )
        else:
            boundary([a1, c1])
    rows, cotangent = bundle[:tokens], bundle[tokens : 2 * tokens]
    ids = bundle[2 * tokens, :length].astype(jnp.int32)
    core1 = [Lane(a1.value, [core_step()]), Lane(c1.value, [core_step()])]
    start(*core1)
    boundary(core1)
    aligned = qkv_rows % 16 == 0 and out_rows % 16 == 0
    count = 2 * lax.axis_size("chip")
    pad_rows = gains.shape[0]
    if aligned:
        qkv_full, gain_rows = assemble(
            [(0, core1[0].value), (cut1, core1[1].value)],
            [(0, 0, qkv_rows, width, 0), (1, qkv_rows, pad_rows, width, 0)],
            [(count * qkv_rows, width), (count * pad_rows, width)],
        )
    else:
        core = lax.axis_index("core")
        mixed_rows = jnp.concatenate(
            [collapse(both(*lane.value, core, 1)) for lane in core1], 1
        )
        qkv_full = mixed_rows[:, :qkv_rows].reshape(-1, width)
        gain_rows = mixed_rows[:, qkv_rows:]
    gain_rows = gain_rows.reshape(-1, gains.shape[0], width)[:, 0]
    gain_a = gain_rows[:, :gain_cols].reshape(1, width).astype(F32)
    gain_b = gain_rows[:, gain_cols : 2 * gain_cols].reshape(1, width).astype(F32)
    resid = rows.astype(F32)
    packed, h_one = project(rows, gain_a, qkv_full, cos_t, sin_t, members)
    qkv = to_heads(packed)
    if members == 2:
        ids = jnp.where(member == 0, ids, jnp.roll(ids, tokens))
    o_h, lse = attend(qkv, ids, head_dim)
    attn = to_tokens(o_h[None], members)[0]
    (attn, second) = boundary([], attn, second)
    at = [0, out_rows, out_rows + qkv_rows, 2 * out_rows + qkv_rows]
    if aligned and rest % 128 == 0:
        attn_full, mlp_in_full, mlp_out_full = assemble(
            [(0, [second])],
            [
                (0, at[0], out_rows, width, 0),
                (1, at[1], qkv_rows, width, 0),
                (2, at[2], out_rows, width, 0),
                (2, at[3], out_rows, rest, width),
            ],
            [(width, width), (count * qkv_rows, width), (width, hidden_units)],
        )
    else:
        attn_full = second[:, : at[1]].reshape(-1, width)
        mlp_in_full = second[:, at[1] : at[2]].reshape(-1, width)
        mlp_out_full = jnp.concatenate(
            [second[:, at[2] : at[3]], second[:, at[3] :, :rest]], -1
        ).reshape(width, hidden_units)

    resid_two = resid + nt(attn, attn_full)
    norm_b, inv_b = normalize(resid_two)
    h_two = (norm_b * gain_b).astype(BF16)
    up = nt(h_two, mlp_in_full)
    act_in = up[:, :hidden_units]
    gate_in = up[:, hidden_units:]
    activated = gelu_exact(act_in)
    mixed = (activated * gate_in).astype(BF16)
    result = (resid_two + nt(mixed, mlp_out_full)).astype(BF16)

    cot32 = cotangent.astype(F32)
    g_mlp_out = tn(cotangent, mixed).astype(BF16)
    s_mlp_out = Reduce(
        g_mlp_out.reshape(count, -1, hidden_units), out_rows // 2 if paired else 0
    )
    result, cotangent = start_with([s_mlp_out.core], result, cotangent)
    d_mixed = nn(cotangent, mlp_out_full)
    unused, gelu_back = jax.vjp(gelu_exact, act_in)
    d_act = gelu_back(d_mixed * gate_in)[0]
    d_up = jnp.concatenate([d_act, d_mixed * activated], -1).astype(BF16)
    g_mlp_in = tn(d_up, h_two).astype(BF16)
    s_mlp_in = Reduce(g_mlp_in.reshape(count, -1, width), 0)
    ascending = list(range(bits))
    zs_first = ascending[1:] + [0]
    d_up, s_mlp_in.core.value = boundary([s_mlp_out.core], d_up, s_mlp_in.core.value)
    s_mlp_out.open(ascending)
    (d_up,) = start_with([s_mlp_in.core] + s_mlp_out.lanes(), d_up)
    d_h_two = nn(d_up, mlp_in_full)
    g_gain_b = jnp.sum(d_h_two * norm_b, 0)
    d_resid_two = cot32 + norm_back(d_h_two * gain_b, norm_b, inv_b)
    d_two = d_resid_two.astype(BF16)
    d_attn = nn(d_two, attn_full).astype(BF16)
    d_packed = d_attn.reshape(1, tokens, members, width // members).transpose(0, 2, 1, 3)
    d_packed, d_two = boundary([s_mlp_in.core], d_packed, d_two)
    s_mlp_in.open(ascending)
    g_attn_out = tn(d_two, attn).astype(BF16)
    s_attn_out = Reduce(g_attn_out.reshape(count, -1, width), 0)
    do_h = to_heads(d_packed)[0]
    (do_h,) = boundary(s_mlp_out.lanes(), do_h)
    moving = s_mlp_in.lanes() + s_mlp_out.lanes()
    (do_h,) = start_with(moving + [s_attn_out.core], do_h)
    grads = attend_back(qkv, ids, lse, o_h, do_h, cos_h, sin_h, head_dim)
    (grads,) = boundary(s_mlp_out.lanes() + [s_attn_out.core], grads)
    s_attn_out.open(zs_first)
    returned = to_tokens(grads, members)
    start(*s_attn_out.lanes(), *s_mlp_out.lanes())
    moving = moving + s_attn_out.lanes()
    d_qkv = jnp.concatenate([returned[0], returned[1], returned[2]], -1)
    g_qkv = tn(d_qkv, h_one).astype(BF16)
    s_qkv = Reduce(g_qkv.reshape(count, -1, width), pair_rows(qkv_rows))
    d_qkv, s_qkv.core.value, result = boundary(moving, d_qkv, s_qkv.core.value, result)
    d_qkv, result = start_with([s_qkv.core] + moving, d_qkv, result)
    layer_out = lax.ppermute(result, swapped, back)
    d_h_one = nn(d_qkv, qkv_full)
    norm_a, inv_a = normalize(resid)
    g_gain_a = jnp.sum(d_h_one * norm_a, 0)
    input_grad = d_resid_two + norm_back(d_h_one * gain_a, norm_a, inv_a)
    sums = Lane(jnp.stack([g_gain_a, g_gain_b]), total_steps())
    input_grad, totals, layer_out = boundary(
        moving + [s_qkv.core], input_grad.astype(BF16), sums.value, layer_out
    )
    sums.value = totals
    layer_out = layer_out[None]
    s_qkv.open(ascending)
    input_grad = lax.ppermute(input_grad, swapped, back).astype(F32)[None]
    moving = s_qkv.lanes() + moving + [sums]
    drain(*moving)
    gains = sums.value
    offset = (lax.axis_index("chip") * 2 + lax.axis_index("core")) * gain_cols
    gains = lax.dynamic_slice_in_dim(gains, offset, gain_cols, 1)
    return (
        layer_out,
        input_grad,
        s_qkv.close(),
        s_attn_out.close(),
        s_mlp_in.close(),
        s_mlp_out.close(),
        gains[0],
        gains[1],
    )


def solution(mesh):
    fsdp, seq = mesh.shape["fsdp"], mesh.shape["seq"]
    inner = Mesh(
        mesh.devices.reshape(fsdp // 2, 2, 2, seq // 2), ("chip", "core", "xg", "xl")
    )
    rows, parts = ("chip", "core"), ("xg", "xl")
    return jax.shard_map(
        per_device,
        mesh=inner,
        in_specs=(
            P(rows, parts, None),
            P(rows, None),
            P(None, rows),
            P(None, rows),
            P(None, rows),
            P(None, rows),
            P(rows),
            P(rows),
            P(rows, parts, None),
        ),
        out_specs=(
            P(rows, parts, None),
            P(rows, parts, None),
            P(None, rows),
            P(None, rows),
            P(None, rows),
            P(None, rows),
            P(rows),
            P(rows),
        ),
        check_vma=False,
    )
```

```python
import math

import jax
import jax.numpy as jnp
from jax import lax
from jax.experimental import pallas as pl
from jax.experimental.pallas import tpu as pltpu
from jax.sharding import Mesh, PartitionSpec as P

HEADS = 12
rope_base = 160000.0
norm_eps = 1e-05
F32 = jnp.float32
BF16 = jnp.bfloat16


def normalize(values):
    centered = values - jnp.mean(values, -1, keepdims=True)
    inverse = lax.rsqrt(jnp.mean(centered * centered, -1, keepdims=True) + norm_eps)
    return (centered * inverse, inverse)


def norm_back(grad, normed, inverse):
    return inverse * (
        grad
        - jnp.mean(grad, -1, keepdims=True)
        - normed * jnp.mean(grad * normed, -1, keepdims=True)
    )


def gelu_exact(values):
    return jax.nn.gelu(values, approximate=False)


def rope_tables(positions, head_dim, repeats):
    half = head_dim // 2
    inverse = rope_base ** (-(jnp.arange(half).astype(F32) * 2.0 / head_dim))
    angle = positions[:, None] * inverse[None, :]
    repeats = repeats if repeats * head_dim % 128 else 128 // head_dim
    angle = jnp.tile(angle, (1, 2 * repeats))
    return jnp.cos(angle), jnp.sin(angle)


def spread(table, width):
    return jnp.concatenate([table] * (width // table.shape[-1]), -1)


def swap_halves(values, head_dim):
    half = head_dim // 2
    width = values.shape[-1]
    if width % 128 == 0:
        lane = lax.broadcasted_iota(jnp.int32, values.shape, 1)
        low = (lane & (head_dim - 1)) < half
        return jnp.where(
            low, -pltpu.roll(values, width - half, 1), pltpu.roll(values, half, 1)
        )
    pieces = []
    for start in range(0, width, head_dim):
        pieces.append(-values[:, start + half : start + head_dim])
        pieces.append(values[:, start : start + half])
    return jnp.concatenate(pieces, -1)


def vmem_specs(count):
    return [pl.BlockSpec(memory_space=pltpu.VMEM)] * count


PARAMS = dict(vmem_limit_bytes=56 * 1024 * 1024)


def project(rows, gain, weights, cos, sin, members):
    tokens, width = rows.shape
    part = width // members
    head_dim = width // HEADS

    def kernel(rows_ref, gain_ref, w_ref, cos_ref, sin_ref, out_ref, h_ref):
        norm, _ = normalize(rows_ref[...].astype(F32))
        h_ref[...] = (norm * gain_ref[...]).astype(BF16)
        h = h_ref[...]
        cos = spread(cos_ref[...], part)
        sin = spread(sin_ref[...], part)
        for kind in range(3):
            for member in range(members):
                start = kind * width + member * part
                values = lax.dot_general(
                    h, w_ref[start : start + part, :], (((1,), (1,)), ((), ())),
                    preferred_element_type=F32,
                )
                if kind < 2:
                    values = values * cos + swap_halves(values, head_dim) * sin
                out_ref[kind, member] = values.astype(BF16)

    return pl.pallas_call(
        kernel,
        out_shape=(
            jax.ShapeDtypeStruct((3, members, tokens, part), BF16),
            jax.ShapeDtypeStruct((tokens, width), BF16),
        ),
        in_specs=vmem_specs(5),
        out_specs=tuple(vmem_specs(2)),
        compiler_params=pltpu.CompilerParams(**PARAMS),
        name="project",
    )(rows, gain, weights, cos, sin)


def flip(value, axis, bit):
    count = lax.axis_size(axis)
    return lax.ppermute(value, axis, [(i, i ^ (1 << bit)) for i in range(count)])


def bits_of(axis):
    count = lax.axis_size(axis)
    bits = count.bit_length() - 1
    assert count == 1 << bits
    return bits


def after(value, *others):
    return lax.optimization_barrier((value,) + others)[0]


def side(axis, bit=0):
    return (lax.axis_index(axis) >> bit) & 1


def both(value, other, upper, axis):
    upper = upper == 1
    return jnp.stack([jnp.where(upper, other, value), jnp.where(upper, value, other)], axis)


class Lane:
    def __init__(self, value, steps):
        self.value, self.steps, self.pending = value, list(steps), None

    def prepare(self):
        split, self.axis, self.bit, self.join = self.steps.pop(0)
        self.keep, self.sending = split(self.value)

    def launch(self):
        self.pending = flip(self.sending, self.axis, self.bit)

    def start(self):
        self.prepare()
        self.launch()

    def finish(self):
        self.value = self.join(self.keep, self.pending)
        self.pending = None


def boundary(lanes, *values):
    lanes = [lane for lane in lanes if lane is not None and lane.pending is not None]
    out = lax.optimization_barrier(tuple(lane.pending for lane in lanes) + tuple(values))
    for lane, got in zip(lanes, out):
        lane.pending = got
        lane.finish()
    return out[len(lanes) :]


def start(*lanes):
    for lane in lanes:
        if lane is not None and lane.steps and lane.pending is None:
            lane.start()


def start_with(lanes, *values):
    lanes = [lane for lane in lanes if lane is not None and lane.steps and lane.pending is None]
    for lane in lanes:
        lane.prepare()
    out = lax.optimization_barrier(tuple(lane.sending for lane in lanes) + tuple(values))
    for lane, send in zip(lanes, out):
        lane.sending = send
        lane.launch()
    return out[len(lanes) :]


def drain(*lanes):
    while any(lane is not None and lane.steps for lane in lanes):
        start(*lanes)
        boundary(lanes)


def collapse(value):
    return value.reshape((-1,) + value.shape[-2:])


def whole(value):
    return value, value


def gather_steps(order):
    steps, have = [], []
    for bit in order:
        place = sum(other > bit for other in have)
        have.append(bit)
        steps.append(
            (whole, "chip", bit,
             lambda keep, got, bit=bit, place=place: both(keep, got, side("chip", bit), place))
        )
    return steps


def cross_step():
    def join(keep, got):
        pair = both(keep, got, lax.axis_index("xg"), 1)
        return pair.reshape(keep.shape[0], -1, keep.shape[-1])

    return (lambda v: (collapse(v), collapse(v)), "xg", 0, join)


def core_step():
    return (lambda v: (collapse(v), collapse(v)), "core", 0, lambda keep, got: (keep, got))


def add_halves(keep, other):
    return (keep.astype(F32) + other.astype(F32)).astype(BF16)


def halving(axis, bit, place):
    def split(value):
        mine = side(axis, bit)
        return (
            lax.dynamic_index_in_dim(value, mine, place, False),
            lax.dynamic_index_in_dim(value, 1 - mine, place, False),
        )

    return (split, axis, bit, add_halves)


def scatter_steps(order):
    have = list(reversed(range(len(order))))
    steps = []
    for bit in order:
        steps.append(halving("chip", bit, have.index(bit)))
        have.remove(bit)
    return steps


def to_bits(value):
    return value.reshape((2,) * bits_of("chip") + value.shape[-2:])


def sum_steps():
    return [
        (lambda v: whole(v.astype(BF16)), axis, bit,
         lambda keep, got: keep.astype(F32) + got.astype(F32))
        for axis in ("xg", "xl")
        for bit in range(bits_of(axis))
    ]


class Reduce:
    def __init__(self, term, half):
        self.half = half

        pairs = term.reshape((-1, 2) + term.shape[1:])
        self.core = Lane(pairs, [halving("core", 0, 1)])
        self.a = self.b = None

    def open(self, order):
        total = self.core.value
        half = self.half
        near = total.shape[1] - 2 * half
        if near:
            self.a = Lane(to_bits(total[:, :near]), scatter_steps(order) + sum_steps())
        if half:
            plane = lax.axis_index("xg")

            def split(value):
                cut = lambda p: lax.dynamic_slice_in_dim(value, near + p * half, half, 1)
                return cut(plane), cut(1 - plane)

            def join(keep, got):
                return to_bits(add_halves(keep, got))

            self.b = Lane(
                total,
                [(split, "xg", 0, join)]
                + scatter_steps(order)
                + [(whole, "xg", 0, lambda keep, got: both(keep, got, lax.axis_index("xg"), 0))],
            )

    def lanes(self):
        return [self.b, self.a]

    def close(self):
        parts = [
            lane.value.reshape((-1,) + lane.value.shape[-1:]).astype(F32)
            for lane in (self.a, self.b)
            if lane is not None
        ]
        return jnp.concatenate(parts, 0).T


def pair_rows(rows):
    if lax.axis_size("xg") * lax.axis_size("xl") != 2:
        return 0
    return rows // 4 // 16 * 16


def assemble(sources, fields, shapes):
    core = lax.axis_index("core")
    arrays, copies = [], []
    for start, pair in sources:
        count = pair[0].shape[1]
        for which, array in enumerate(pair):
            arrays.append(array)
            for index in range(array.shape[0]):
                for out, first, rows, columns, column in fields:
                    low, high = max(first, start), min(first + rows, start + count)
                    if low < high:
                        copies.append(
                            (len(arrays) - 1, index, low - start, high - low, out,
                             len(pair), which, rows, low - first, columns, column)
                        )

    def kernel(core_ref, *refs):
        ins, outs = refs[: len(arrays)], refs[len(arrays) : -1]
        sems = refs[-1]
        started = []
        for number, copy in enumerate(copies):
            source, index, low, size, out, pairs, which, rows, offset, columns, column = copy
            at = index
            if pairs == 2:
                at = 2 * index + (core_ref[0] if which == 0 else 1 - core_ref[0])
            base = at * rows + offset
            if pairs == 2:
                base = pl.multiple_of(base, 16)
            handle = pltpu.make_async_copy(
                ins[source].at[index, low : low + size, :columns],
                outs[out].at[pl.ds(base, size), column : column + columns],
                sems.at[number],
            )
            handle.start()
            started.append(handle)
        for handle in started:
            handle.wait()

    return pl.pallas_call(
        kernel,
        out_shape=tuple(jax.ShapeDtypeStruct(shape, BF16) for shape in shapes),
        in_specs=[pl.BlockSpec(memory_space=pltpu.SMEM)]
        + [pl.BlockSpec(memory_space=pl.ANY)] * len(arrays),
        out_specs=tuple(vmem_specs(len(shapes))),
        scratch_shapes=[pltpu.SemaphoreType.DMA((len(copies),))],
        compiler_params=pltpu.CompilerParams(**PARAMS),
        name="assemble",
    )(core[None].astype(jnp.int32), *arrays)


def total_steps():
    return [
        (whole, axis, bit, lambda keep, got: keep + got)
        for axis in ("core", "chip", "xg", "xl")
        for bit in range(bits_of(axis))
    ]


def attend(qkv, ids, head_dim):
    length, part = qkv.shape[1:]
    heads = part // head_dim
    scale = head_dim ** (-0.5)

    def kernel(qkv_ref, row_ref, col_ref, out_ref, lse_ref):
        keep = col_ref[...] == row_ref[...]
        for head in range(heads):
            lanes = slice(head * head_dim, (head + 1) * head_dim)
            scores = lax.dot_general(
                qkv_ref[0, :, lanes], qkv_ref[1, :, lanes], (((1,), (1,)), ((), ())),
                preferred_element_type=F32,
            ) * scale
            scores = jnp.where(keep, scores, -jnp.inf)
            top = jnp.max(scores, -1, keepdims=True)
            weight = jnp.exp(scores - top)
            total = jnp.sum(weight, -1, keepdims=True)
            out = jnp.dot(weight.astype(BF16), qkv_ref[2, :, lanes], preferred_element_type=F32)
            out_ref[:, lanes] = (out / total).astype(BF16)
            lse_ref[:, head : head + 1] = top + jnp.log(total)

    return pl.pallas_call(
        kernel,
        out_shape=(
            jax.ShapeDtypeStruct((length, part), BF16),
            jax.ShapeDtypeStruct((length, heads), F32),
        ),
        in_specs=vmem_specs(3),
        out_specs=tuple(vmem_specs(2)),
        compiler_params=pltpu.CompilerParams(**PARAMS),
        name="attend",
    )(qkv, ids[None, :], ids[:, None])


def attend_back(qkv, ids, lse, out, d_out, cos, sin, head_dim):
    length, part = qkv.shape[1:]
    heads = part // head_dim
    scale = head_dim ** (-0.5)

    def kernel(qkv_ref, row_ref, col_ref, lse_ref, out_ref, do_ref, cos_ref, sin_ref, grad_ref, dq_ref, dk_ref):
        keep = col_ref[...] == row_ref[...]
        for head in range(heads):
            lanes = slice(head * head_dim, (head + 1) * head_dim)
            query = qkv_ref[0, :, lanes]
            key = qkv_ref[1, :, lanes]
            d_head = do_ref[:, lanes]
            scores = lax.dot_general(
                query, key, (((1,), (1,)), ((), ())), preferred_element_type=F32
            ) * scale
            prob = jnp.where(keep, jnp.exp(scores - lse_ref[:, head : head + 1]), 0.0)
            d_prob = lax.dot_general(
                d_head, qkv_ref[2, :, lanes], (((1,), (1,)), ((), ())),
                preferred_element_type=F32,
            )
            delta = jnp.sum(d_head.astype(F32) * out_ref[:, lanes].astype(F32), -1, keepdims=True)
            d_score = (prob * (d_prob - delta)).astype(BF16)
            grad_ref[2, :, lanes] = lax.dot_general(
                prob.astype(BF16), d_head, (((0,), (0,)), ((), ())), preferred_element_type=F32
            ).astype(BF16)
            dq_ref[:, lanes] = jnp.dot(d_score, key, preferred_element_type=F32) * scale
            dk_ref[:, lanes] = lax.dot_general(
                d_score, query, (((0,), (0,)), ((), ())), preferred_element_type=F32
            ) * scale
        for kind, ref in enumerate((dq_ref, dk_ref)):
            values = ref[...]
            cos = spread(cos_ref[...], part)
            sin = spread(sin_ref[...], part)
            turned = values * cos - swap_halves(values * sin, head_dim)
            grad_ref[kind] = turned.astype(BF16)

    return pl.pallas_call(
        kernel,
        out_shape=jax.ShapeDtypeStruct((3, length, part), BF16),
        in_specs=vmem_specs(8),
        out_specs=vmem_specs(1)[0],
        scratch_shapes=[pltpu.VMEM((length, part), F32)] * 2,
        compiler_params=pltpu.CompilerParams(**PARAMS),
        name="attend_back",
    )(qkv, ids[None, :], ids[:, None], lse, out, d_out, cos, sin)


def to_heads(packed):
    members = packed.shape[1]
    if members == 2:
        core = lax.axis_index("core")
        mine = lax.dynamic_index_in_dim(packed, core, 1, False)
        send = lax.dynamic_index_in_dim(packed, 1 - core, 1, False)
        return jnp.concatenate([mine, flip(send, "core", 0)], 1)
    got = lax.all_to_all(packed, GROUP, split_axis=1, concat_axis=1, tiled=True)
    return got.reshape(got.shape[0], -1, got.shape[-1])


def to_tokens(values, members):
    count, length, part = values.shape
    tokens = length // members
    if members == 2:
        first = lax.axis_index("core") == 0
        mine = values[:, :tokens]
        other = flip(values[:, tokens:], "core", 0)
        return jnp.where(
            first, jnp.concatenate([mine, other], -1), jnp.concatenate([other, mine], -1)
        )
    got = values.reshape(count, members, tokens, part)
    got = lax.all_to_all(got, GROUP, split_axis=1, concat_axis=1, tiled=True)
    return got.transpose(0, 2, 1, 3).reshape(count, tokens, members * part)


def nt(left, right):
    return lax.dot_general(left, right, (((1,), (1,)), ((), ())), preferred_element_type=F32)


def tn(left, right):
    return lax.dot_general(left, right, (((0,), (0,)), ((), ())), preferred_element_type=F32)


def nn(left, right):
    return jnp.dot(left, right, preferred_element_type=F32)


GROUP = ("xl", "core")


def erf_gelu(values):
    cdf = 0.5 * (1.0 + lax.erf(values * (0.5**0.5)))
    slope = cdf + values * jnp.exp(-0.5 * values * values) * ((2.0 * math.pi) ** -0.5)
    return values * cdf, slope


def choose(first, yes, no):
    pl.when(first)(yes)
    pl.when(jnp.logical_not(first))(no)


def kernel_call(kernel, name, outs, specs, scratch, core, *args):
    return pl.pallas_call(
        kernel,
        out_shape=tuple(jax.ShapeDtypeStruct(shape, kind) for shape, kind in outs),
        in_specs=[pl.BlockSpec(memory_space=pltpu.SMEM)] + specs,
        out_specs=tuple(vmem_specs(len(outs))),
        scratch_shapes=scratch,
        compiler_params=pltpu.CompilerParams(**PARAMS),
        name=name,
    )(core[None].astype(jnp.int32), *args)


def store_half(core, member, mine, send, at, value):
    def keep_it():
        mine[at] = value

    def send_it():
        send[at] = value

    choose(core == member, keep_it, send_it)


def store_shards(core, keep, send, value, base, rows, offset, lanes):
    done = 0
    while done < value.shape[0]:
        shard, inside = divmod(base + done, rows)
        size = min(rows - inside, value.shape[0] - done)
        at = (shard // 2, slice(offset + inside, offset + inside + size), lanes)
        store_half(core, shard % 2, keep, send, at, value[done : done + size])
        done += size


def pair_project(core, bundle, gain, weights, cos, sin, tokens):
    width = bundle.shape[1]
    part = width // 2
    head_dim = width // HEADS

    def kernel(core_ref, rows_ref, gain_ref, w_ref, cos_ref, sin_ref, mine_ref, send_ref, h_ref):
        norm, _ = normalize(rows_ref[:tokens].astype(F32))
        h_ref[...] = (norm * gain_ref[...]).astype(BF16)
        h = h_ref[...]
        cos = spread(cos_ref[:tokens], part)
        sin = spread(sin_ref[:tokens], part)
        for kind in range(3):
            for member in range(2):
                begin = kind * width + member * part
                values = nt(h, w_ref[begin : begin + part, :])
                if kind < 2:
                    values = values * cos + swap_halves(values, head_dim) * sin
                store_half(core_ref[0], member, mine_ref, send_ref, kind, values.astype(BF16))

    half = ((3, tokens, part), BF16)
    return kernel_call(
        kernel, "project", [half, half, ((tokens, width), BF16)], vmem_specs(5), [],
        core, bundle, gain, weights, cos, sin,
    )


def joined(first, second, lanes, kind=None):
    if kind is None:
        return jnp.concatenate([first[:, lanes], second[:, lanes]], 0)
    return jnp.concatenate([first[kind, :, lanes], second[kind, :, lanes]], 0)


def pair_attend(core, mine, other, ids, head_dim):
    tokens, part = mine.shape[1:]
    heads = part // head_dim
    scale = head_dim ** (-0.5)

    def kernel(core_ref, mine_ref, other_ref, row_ref, col_ref, out_ref, send_ref, lse_ref):
        keep = col_ref[...] == row_ref[...]
        for head in range(heads):
            lanes = slice(head * head_dim, (head + 1) * head_dim)
            query, key, value = (joined(mine_ref, other_ref, lanes, kind) for kind in range(3))
            scores = jnp.where(keep, nt(query, key) * scale, -jnp.inf)
            top = jnp.max(scores, -1, keepdims=True)
            weight = jnp.exp(scores - top)
            total = jnp.sum(weight, -1, keepdims=True)
            out = (nn(weight.astype(BF16), value) / total).astype(BF16)
            out_ref[:, lanes] = out[:tokens]
            send_ref[:, lanes] = out[tokens:]
            lse_ref[:, head : head + 1] = top + jnp.log(total)

    half = ((tokens, part), BF16)
    return kernel_call(
        kernel, "attend", [half, half, ((2 * tokens, heads), F32)], vmem_specs(4), [],
        core, mine, other, ids[None, :], ids[:, None],
    )


def pair_mlp(core, mine, other, bundle, gain, second, at, rest):
    tokens, part = mine.shape
    width = 2 * part
    shards = second.shape[0]
    out_rows, in_rows = at[1], at[2] - at[1]
    hidden = shards * in_rows // 2
    group = second.shape[1]
    high = slice(width, width + rest)

    def kernel(
        core_ref, mine_ref, other_ref, bundle_ref, gain_ref, second_ref,
        layer_ref, resid_ref, dmine_ref, dsend_ref, keep_ref, send_ref,
        attn_ref, wo_ref, wi_ref, wm_ref, sems,
    ):
        here = core_ref[0]

        def copies(stage):
            made = []
            for shard in range(shards):
                fields = {
                    0: [(wo_ref, at[0], out_rows, slice(0, width), slice(0, width))],
                    1: [(wi_ref, at[1], in_rows, slice(0, width), slice(0, width))],
                    2: [
                        (wm_ref, at[2], out_rows, slice(0, width), slice(0, width)),
                        (wm_ref, at[3], out_rows, slice(0, rest), high),
                    ],
                }[stage]
                for index, (ref, begin, rows, source, target) in enumerate(fields):
                    made.append(
                        pltpu.make_async_copy(
                            second_ref.at[shard, begin : begin + rows, source],
                            ref.at[shard * rows : (shard + 1) * rows, target],
                            sems.at[stage + index, shard],
                        )
                    )
            return made

        stages = [copies(stage) for stage in range(3)]
        for stage in stages:
            for copy in stage:
                copy.start()

        def left():
            attn_ref[:, :part] = mine_ref[...]
            attn_ref[:, part:] = other_ref[...]

        def right():
            attn_ref[:, :part] = other_ref[...]
            attn_ref[:, part:] = mine_ref[...]

        choose(here == 0, left, right)
        attn = attn_ref[...]
        cot = bundle_ref[tokens : 2 * tokens]
        for copy in stages[0]:
            copy.wait()
        two = bundle_ref[:tokens].astype(F32) + nt(attn, wo_ref[...])
        norm_b, inv_b = normalize(two)
        h_two = (norm_b * gain_ref[...]).astype(BF16)
        for copy in stages[1]:
            copy.wait()
        act = nt(h_two, wi_ref[:hidden])
        gate = nt(h_two, wi_ref[hidden:])
        activated, slope = erf_gelu(act)
        mixed = (activated * gate).astype(BF16)
        for copy in stages[2]:
            copy.wait()
        layer_ref[...] = (two + nt(mixed, wm_ref[...])).astype(BF16)
        d_mixed = nn(cot, wm_ref[...])
        d_act = (d_mixed * gate * slope).astype(BF16)
        d_gate = (d_mixed * activated).astype(BF16)
        d_h_two = nn(d_act, wi_ref[:hidden]) + nn(d_gate, wi_ref[hidden:])
        d_gain = jnp.sum(d_h_two * norm_b, 0, keepdims=True)
        d_two32 = cot.astype(F32) + norm_back(d_h_two * gain_ref[...], norm_b, inv_b)
        resid_ref[...] = d_two32
        d_two = d_two32.astype(BF16)
        d_attn = nn(d_two, wo_ref[...]).astype(BF16)
        for member in range(2):
            store_half(
                here, member, dmine_ref, dsend_ref, slice(None),
                d_attn[:, member * part : (member + 1) * part],
            )
        every = slice(0, width)

        def put(value, base, rows, offset, lanes):
            store_shards(here, keep_ref, send_ref, value.astype(BF16), base, rows, offset, lanes)

        block = part
        for begin in range(0, width, block):
            columns = slice(begin, begin + block)
            term = tn(cot[:, columns], mixed)
            put(term[:, :width], begin, out_rows, at[2], every)
            put(term[:, width:], begin, out_rows, at[3], slice(0, rest))
            put(tn(d_two[:, columns], attn), begin, out_rows, at[0], every)
        for begin in range(0, hidden, block):
            columns = slice(begin, begin + block)
            put(tn(d_act[:, columns], h_two), begin, in_rows, at[1], every)
            put(tn(d_gate[:, columns], h_two), hidden + begin, in_rows, at[1], every)
        spare = width - rest
        line = lax.broadcasted_iota(jnp.int32, (out_rows, spare), 0)
        fill = jnp.zeros((out_rows, spare), F32)
        for index in range(width // spare):
            piece = d_gain[:, index * spare : (index + 1) * spare]
            fill = jnp.where(line == index, piece, fill)
        fill = fill.astype(BF16)
        for chip in range(shards // 2):
            keep_ref[chip, at[3] : at[3] + out_rows, rest:] = fill
            send_ref[chip, at[3] : at[3] + out_rows, rest:] = fill

    half = ((tokens, part), BF16)
    grads = ((shards // 2, group, width), BF16)
    return kernel_call(
        kernel, "mlp",
        [((tokens, width), BF16), ((tokens, width), F32), half, half, grads, grads],
        vmem_specs(4) + [pl.BlockSpec(memory_space=pl.ANY)],
        [
            pltpu.VMEM((tokens, width), BF16),
            pltpu.VMEM((width, width), BF16),
            pltpu.VMEM((2 * hidden, width), BF16),
            pltpu.VMEM((width, hidden), BF16),
            pltpu.SemaphoreType.DMA((4, shards)),
        ],
        core, mine, other, bundle, gain, second,
    )


def pair_attend_back(core, mine, other, ids, lse, out, sent, d_mine, d_other, cos, sin, head_dim):
    tokens, part = mine.shape[1:]
    heads = part // head_dim
    scale = head_dim ** (-0.5)

    def kernel(
        core_ref, mine_ref, other_ref, row_ref, col_ref, lse_ref, out_ref, sent_ref,
        dm_ref, do_ref, cos_ref, sin_ref, keep_ref, send_ref, dq_ref, dk_ref,
    ):
        keep = col_ref[...] == row_ref[...]
        for head in range(heads):
            lanes = slice(head * head_dim, (head + 1) * head_dim)
            query, key, value = (joined(mine_ref, other_ref, lanes, kind) for kind in range(3))
            d_head = joined(dm_ref, do_ref, lanes)
            prob = jnp.where(
                keep, jnp.exp(nt(query, key) * scale - lse_ref[:, head : head + 1]), 0.0
            )
            d_prob = nt(d_head, value)
            delta = jnp.sum(
                d_head.astype(F32) * joined(out_ref, sent_ref, lanes).astype(F32),
                -1, keepdims=True,
            )
            d_score = (prob * (d_prob - delta)).astype(BF16)
            d_value = tn(prob.astype(BF16), d_head).astype(BF16)
            keep_ref[2, :, lanes] = d_value[:tokens]
            send_ref[2, :, lanes] = d_value[tokens:]
            dq_ref[:, lanes] = nn(d_score, key) * scale
            dk_ref[:, lanes] = tn(d_score, query) * scale
        cos = spread(cos_ref[...], part)
        sin = spread(sin_ref[...], part)
        for kind, ref in enumerate((dq_ref, dk_ref)):
            values = ref[...]
            turned = (values * cos - swap_halves(values * sin, head_dim)).astype(BF16)
            keep_ref[kind] = turned[:tokens]
            send_ref[kind] = turned[tokens:]

    half = ((3, tokens, part), BF16)
    return kernel_call(
        kernel, "attend_back", [half, half], vmem_specs(11),
        [pltpu.VMEM((2 * tokens, part), F32)] * 2,
        core, mine, other, ids[None, :], ids[:, None], lse, out, sent, d_mine, d_other, cos, sin,
    )


def pair_final(core, mine, other, h_one, bundle, gain, weights, resid, rows):
    tokens, part = mine.shape[1:]
    width = 2 * part
    chips = 3 * width // rows // 2

    def kernel(
        core_ref, mine_ref, other_ref, h_ref, bundle_ref, gain_ref, w_ref, resid_ref,
        grad_ref, keep_ref, send_ref, d_ref,
    ):
        here = core_ref[0]
        for kind in range(3):
            for member in range(2):
                begin = kind * width + member * part

                def own(begin=begin, kind=kind):
                    d_ref[:, begin : begin + part] = mine_ref[kind]

                def theirs(begin=begin, kind=kind):
                    d_ref[:, begin : begin + part] = other_ref[kind]

                choose(here == member, own, theirs)
        h = h_ref[...]
        for begin in range(0, 3 * width, part):
            term = tn(d_ref[:, begin : begin + part], h).astype(BF16)
            store_shards(here, keep_ref, send_ref, term, begin, rows, 0, slice(0, width))
        d_h = nn(d_ref[...], w_ref[...])
        norm, inv = normalize(bundle_ref[:tokens].astype(F32))
        d_gain = jnp.sum(d_h * norm, 0, keepdims=True)
        grad_ref[...] = (
            resid_ref[...] + norm_back(d_h * gain_ref[...], norm, inv)
        ).astype(BF16)
        fill = jnp.broadcast_to(d_gain, (16, width)).astype(BF16)
        for chip in range(chips):
            keep_ref[chip, rows : rows + 16, :] = fill
            send_ref[chip, rows : rows + 16, :] = fill

    grads = ((chips, rows + 16, width), BF16)
    return kernel_call(
        kernel, "final", [((tokens, width), BF16), grads, grads], vmem_specs(7),
        [pltpu.VMEM((tokens, 3 * width), BF16)],
        core, mine, other, h_one, bundle, gain, weights, resid,
    )


class PairReduce(Reduce):
    def __init__(self, keep, send, half):
        self.half = half
        self.core = Lane(None, [(lambda value: (keep, send), "core", 0, add_halves)])
        self.a = self.b = None


def pair_steps(
    bundle, qkv_full, gain_a, gain_b, second, cos, sin, ids, at, rest, head_dim, swapped, back
):
    core = lax.axis_index("core")
    chips = lax.axis_size("chip")
    tokens = ids.shape[0] // 2
    width = bundle.shape[1]
    qkv_rows, out_rows = at[2] - at[1], at[1]
    ascending = list(range(bits_of("chip")))
    mine, send, h_one = pair_project(core, bundle, gain_a, qkv_full, cos, sin, tokens)
    other = flip(send, "core", 0)
    out, sent, lse = pair_attend(core, mine, other, ids, head_dim)
    theirs = flip(sent, "core", 0)
    theirs, second = boundary([], theirs, second)
    layer, resid, d_mine, d_send, keep, give = pair_mlp(
        core, out, theirs, bundle, gain_b, second, at, rest
    )
    s_mlp = PairReduce(keep, give, pair_rows(second.shape[1]))
    d_other = flip(d_send, "core", 0)
    start(s_mlp.core)
    g_mine, g_send = pair_attend_back(
        core, mine, other, ids, lse, out, sent, d_mine, d_other, cos, sin, head_dim
    )
    (g_mine, g_send) = boundary([s_mlp.core], g_mine, g_send)
    g_other = flip(g_send, "core", 0)
    s_mlp.open(ascending)
    (g_mine,) = start_with(s_mlp.lanes(), g_mine)
    in_grad, keep, give = pair_final(
        core, g_mine, g_other, h_one, bundle, gain_a, qkv_full, resid, qkv_rows
    )
    s_qkv = PairReduce(keep, give, pair_rows(qkv_rows + 16))
    start(s_qkv.core)
    boundary([s_qkv.core] + s_mlp.lanes())
    s_qkv.open(ascending)
    layer = after(layer, s_qkv.core.value)
    layer_out = lax.ppermute(layer, swapped, back)
    input_grad = lax.ppermute(in_grad, swapped, back)
    drain(*(s_qkv.lanes() + s_mlp.lanes()))
    mlp, qkv = s_mlp.close().T, s_qkv.close().T
    spare = width - rest
    gain_two = mlp[at[3] : at[3] + width // spare, rest:].reshape(width)
    gain_one = qkv[qkv_rows]
    cols = width // (2 * chips)
    offset = (lax.axis_index("chip") * 2 + core) * cols
    return (
        layer_out[None],
        input_grad.astype(F32)[None],
        qkv[:qkv_rows].T,
        mlp[: at[1]].T,
        mlp[at[1] : at[2]].T,
        jnp.concatenate([mlp[at[2] : at[3]], mlp[at[3] :, :rest]], -1).T,
        lax.dynamic_slice_in_dim(gain_one, offset, cols, 0),
        lax.dynamic_slice_in_dim(gain_two, offset, cols, 0),
    )


def per_device(
    hidden_in,
    doc_ids,
    w_qkv,
    w_attn_out,
    w_mlp_in,
    w_mlp_out,
    norm_gain_one,
    norm_gain_two,
    out_grad,
):
    parts = lax.axis_size("xg") * lax.axis_size("xl")
    swap = [
        (core * parts + x, (x % 2) * parts + (core * parts + x) // 2)
        for core in range(2)
        for x in range(parts)
    ]
    back = [(there, here) for here, there in swap]
    swapped = ("core", "xg", "xl")
    tokens, width = hidden_in.shape[1:]
    length = doc_ids.shape[1]
    id_row = jnp.pad(doc_ids.astype(BF16), ((0, 15), (0, width - length)))
    bundle = lax.ppermute(
        jnp.concatenate([hidden_in[0], out_grad[0], id_row], 0), swapped, swap
    )
    head_dim = width // HEADS
    member = lax.axis_index("xl") * 2 + lax.axis_index("core")
    plane = lax.axis_index("xg")

    qkv_rows = w_qkv.shape[1]
    out_rows = w_attn_out.shape[1]
    gain_cols = norm_gain_one.shape[0]
    hidden_units = w_mlp_out.shape[0]
    gains = jnp.concatenate([norm_gain_one, norm_gain_two])[None]
    gains = jnp.pad(gains, ((0, 15), (0, width - 2 * gain_cols)))
    mlp_out_t = w_mlp_out.T
    rest = hidden_units - width
    second_shard = jnp.concatenate(
        [w_attn_out.T, w_mlp_in.T, mlp_out_t[:, :width],
         jnp.pad(mlp_out_t[:, width:], ((0, 0), (0, width - rest)))], 0
    )
    second = lax.all_gather(second_shard, ("chip", "core"), axis=0, tiled=False)
    first_shard = jnp.concatenate([w_qkv.T, gains], 0)
    bits = bits_of("chip")
    z_first = list(reversed(range(bits)))
    y_first = [0] + z_first[:-1]
    members = parts
    per_member = HEADS // members
    paired = parts == 2

    cut1 = first_shard.shape[0] * 3 // 5 // 16 * 16
    a1 = Lane(first_shard[:cut1], gather_steps(z_first))
    c1 = Lane(first_shard[cut1:], gather_steps(y_first))
    places = jnp.arange(length)
    if members == 2:
        places = (places + member * tokens) % length
    cos_h, sin_h = rope_tables(places.astype(F32), head_dim, per_member)
    if members == 2:
        cos_t, sin_t = cos_h[:tokens], sin_h[:tokens]
    else:
        cos_t, sin_t = rope_tables(
            (member * tokens + jnp.arange(tokens)).astype(F32), head_dim, per_member
        )
    for phase in range(bits):
        start(a1, c1)
        if phase == 0:
            boundary([a1, c1])
        elif phase == 1:
            cos_h, sin_h, bundle = boundary([a1, c1], cos_h, sin_h, bundle)
        else:
            boundary([a1, c1])
    rows, cotangent = bundle[:tokens], bundle[tokens : 2 * tokens]
    ids = bundle[2 * tokens, :length].astype(jnp.int32)
    core1 = [Lane(a1.value, [core_step()]), Lane(c1.value, [core_step()])]
    start(*core1)
    boundary(core1)
    aligned = qkv_rows % 16 == 0 and out_rows % 16 == 0
    count = 2 * lax.axis_size("chip")
    pad_rows = gains.shape[0]
    if aligned:
        qkv_full, gain_rows = assemble(
            [(0, core1[0].value), (cut1, core1[1].value)],
            [(0, 0, qkv_rows, width, 0), (1, qkv_rows, pad_rows, width, 0)],
            [(count * qkv_rows, width), (count * pad_rows, width)],
        )
    else:
        core = lax.axis_index("core")
        mixed_rows = jnp.concatenate(
            [collapse(both(*lane.value, core, 1)) for lane in core1], 1
        )
        qkv_full = mixed_rows[:, :qkv_rows].reshape(-1, width)
        gain_rows = mixed_rows[:, qkv_rows:]
    gain_rows = gain_rows.reshape(-1, gains.shape[0], width)[:, 0]
    gain_a = gain_rows[:, :gain_cols].reshape(1, width).astype(F32)
    gain_b = gain_rows[:, gain_cols : 2 * gain_cols].reshape(1, width).astype(F32)
    at = [0, out_rows, out_rows + qkv_rows, 2 * out_rows + qkv_rows]
    if paired and aligned and width % 256 == 0 and rest % 128 == 0 and rest < width:
        ids = jnp.where(member == 0, ids, jnp.roll(ids, tokens))
        return pair_steps(
            bundle, qkv_full, gain_a, gain_b, second, cos_h, sin_h, ids, at, rest, head_dim,
            swapped, back,
        )
    resid = rows.astype(F32)
    packed, h_one = project(rows, gain_a, qkv_full, cos_t, sin_t, members)
    qkv = to_heads(packed)
    if members == 2:
        ids = jnp.where(member == 0, ids, jnp.roll(ids, tokens))
    o_h, lse = attend(qkv, ids, head_dim)
    attn = to_tokens(o_h[None], members)[0]
    (attn, second) = boundary([], attn, second)
    if aligned and rest % 128 == 0:
        attn_full, mlp_in_full, mlp_out_full = assemble(
            [(0, [second])],
            [
                (0, at[0], out_rows, width, 0),
                (1, at[1], qkv_rows, width, 0),
                (2, at[2], out_rows, width, 0),
                (2, at[3], out_rows, rest, width),
            ],
            [(width, width), (count * qkv_rows, width), (width, hidden_units)],
        )
    else:
        attn_full = second[:, : at[1]].reshape(-1, width)
        mlp_in_full = second[:, at[1] : at[2]].reshape(-1, width)
        mlp_out_full = jnp.concatenate(
            [second[:, at[2] : at[3]], second[:, at[3] :, :rest]], -1
        ).reshape(width, hidden_units)

    resid_two = resid + nt(attn, attn_full)
    norm_b, inv_b = normalize(resid_two)
    h_two = (norm_b * gain_b).astype(BF16)
    up = nt(h_two, mlp_in_full)
    act_in = up[:, :hidden_units]
    gate_in = up[:, hidden_units:]
    activated = gelu_exact(act_in)
    mixed = (activated * gate_in).astype(BF16)
    result = (resid_two + nt(mixed, mlp_out_full)).astype(BF16)

    cot32 = cotangent.astype(F32)
    g_mlp_out = tn(cotangent, mixed).astype(BF16)
    s_mlp_out = Reduce(
        g_mlp_out.reshape(count, -1, hidden_units), out_rows // 2 if paired else 0
    )
    result, cotangent = start_with([s_mlp_out.core], result, cotangent)
    d_mixed = nn(cotangent, mlp_out_full)
    unused, gelu_back = jax.vjp(gelu_exact, act_in)
    d_act = gelu_back(d_mixed * gate_in)[0]
    d_up = jnp.concatenate([d_act, d_mixed * activated], -1).astype(BF16)
    g_mlp_in = tn(d_up, h_two).astype(BF16)
    s_mlp_in = Reduce(g_mlp_in.reshape(count, -1, width), 0)
    ascending = list(range(bits))
    zs_first = ascending[1:] + [0]
    d_up, s_mlp_in.core.value = boundary([s_mlp_out.core], d_up, s_mlp_in.core.value)
    s_mlp_out.open(ascending)
    (d_up,) = start_with([s_mlp_in.core] + s_mlp_out.lanes(), d_up)
    d_h_two = nn(d_up, mlp_in_full)
    g_gain_b = jnp.sum(d_h_two * norm_b, 0)
    d_resid_two = cot32 + norm_back(d_h_two * gain_b, norm_b, inv_b)
    d_two = d_resid_two.astype(BF16)
    d_attn = nn(d_two, attn_full).astype(BF16)
    d_packed = d_attn.reshape(1, tokens, members, width // members).transpose(0, 2, 1, 3)
    d_packed, d_two = boundary([s_mlp_in.core], d_packed, d_two)
    s_mlp_in.open(ascending)
    g_attn_out = tn(d_two, attn).astype(BF16)
    s_attn_out = Reduce(g_attn_out.reshape(count, -1, width), 0)
    do_h = to_heads(d_packed)[0]
    (do_h,) = boundary(s_mlp_out.lanes(), do_h)
    moving = s_mlp_in.lanes() + s_mlp_out.lanes()
    (do_h,) = start_with(moving + [s_attn_out.core], do_h)
    grads = attend_back(qkv, ids, lse, o_h, do_h, cos_h, sin_h, head_dim)
    (grads,) = boundary(s_mlp_out.lanes() + [s_attn_out.core], grads)
    s_attn_out.open(zs_first)
    returned = to_tokens(grads, members)
    start(*s_attn_out.lanes(), *s_mlp_out.lanes())
    moving = moving + s_attn_out.lanes()
    d_qkv = jnp.concatenate([returned[0], returned[1], returned[2]], -1)
    g_qkv = tn(d_qkv, h_one).astype(BF16)
    s_qkv = Reduce(g_qkv.reshape(count, -1, width), pair_rows(qkv_rows))
    d_qkv, s_qkv.core.value, result = boundary(moving, d_qkv, s_qkv.core.value, result)
    d_qkv, result = start_with([s_qkv.core] + moving, d_qkv, result)
    layer_out = lax.ppermute(result, swapped, back)
    d_h_one = nn(d_qkv, qkv_full)
    norm_a, inv_a = normalize(resid)
    g_gain_a = jnp.sum(d_h_one * norm_a, 0)
    input_grad = d_resid_two + norm_back(d_h_one * gain_a, norm_a, inv_a)
    sums = Lane(jnp.stack([g_gain_a, g_gain_b]), total_steps())
    input_grad, totals, layer_out = boundary(
        moving + [s_qkv.core], input_grad.astype(BF16), sums.value, layer_out
    )
    sums.value = totals
    layer_out = layer_out[None]
    s_qkv.open(ascending)
    input_grad = lax.ppermute(input_grad, swapped, back).astype(F32)[None]
    moving = s_qkv.lanes() + moving + [sums]
    drain(*moving)
    gains = sums.value
    offset = (lax.axis_index("chip") * 2 + lax.axis_index("core")) * gain_cols
    gains = lax.dynamic_slice_in_dim(gains, offset, gain_cols, 1)
    return (
        layer_out,
        input_grad,
        s_qkv.close(),
        s_attn_out.close(),
        s_mlp_in.close(),
        s_mlp_out.close(),
        gains[0],
        gains[1],
    )


def solution(mesh):
    fsdp, seq = mesh.shape["fsdp"], mesh.shape["seq"]
    inner = Mesh(
        mesh.devices.reshape(fsdp // 2, 2, 2, seq // 2), ("chip", "core", "xg", "xl")
    )
    rows, parts = ("chip", "core"), ("xg", "xl")
    return jax.shard_map(
        per_device,
        mesh=inner,
        in_specs=(
            P(rows, parts, None),
            P(rows, None),
            P(None, rows),
            P(None, rows),
            P(None, rows),
            P(None, rows),
            P(rows),
            P(rows),
            P(rows, parts, None),
        ),
        out_specs=(
            P(rows, parts, None),
            P(rows, parts, None),
            P(None, rows),
            P(None, rows),
            P(None, rows),
            P(None, rows),
            P(rows),
            P(rows),
        ),
        check_vma=False,
    )
```
